32 devices in a mesh: tm: 2 (over y), height: 16 (over z, x, core).
Axes of the slice: x: 2, y: 2, z: 4, core: 2. Of those that a mesh axis runs over, the one named last changes fastest.
Arguments:
- latents: bfloat16 [2, 4, 32, 128, 512], P(None, 'tm', 'height'), may hold values from -6 to 6
- norm_gain: float32 [512], replicated, may hold values from 0.25 to 1.75
- spatial_weight: bfloat16 [3, 3, 512, 512], replicated, may hold values from -0.09375 to 0.09375
- temporal_weight: float32 [3, 512], replicated, may hold values from -3 to 3
- codebooks: bfloat16 [2, 32768, 512], P(None, 'height'), may hold values from -6 to 6
- ema_counts: float32 [2, 32768], P(None, 'height'), may hold values from 0.3 to 30
- ema_sums: float32 [2, 32768, 512], P(None, 'height', 'tm'), may hold values from -6 to 6
- decay: float32 [2], replicated, may hold values from 0.6 to 0.9
- codes_first: int32 [2, 4, 32, 128], P(None, 'tm', 'height'), may hold values from 0 to 32767, as said below
- codes_second: int32 [2, 4, 32, 128], P(None, 'tm', 'height'), may hold values from 0 to 32767, as said below
Outputs:
- ema_counts_new: float32 [2, 32768], P(None, 'height')
- ema_sums_new: float32 [2, 32768, 512], P(None, 'height', 'tm')
- error: float32 [2, 4, 32, 128], P(None, 'tm', 'height')
The draws below stay inside these ranges and needn't reach their ends.
Inputs may be any that keep to these rules, and one draw needn't show every extreme that they name: `codes_first`: the codes of index o of height are o * 2048 to (o + 1) * 2048 - 1. In the latents of one device (all 2 clips over its 2 frames and 2 rows) at most 128 name codes of one owner o, and in every draw, for every index of tm, some owner gets exactly 128 from every device of that index. `codes_second`: as for codes_first, drawn independently.
All inputs are finite; a program needn't handle non-finite values.
Results may differ from the reference program's by a relative error of at most 0.0031.
Values may be sent and summed in bfloat16 or wider, within the bound.
A program may use at most 128 MiB of HBM per device.

```python
import math
import jax
import jax.numpy as jnp
from jax import lax

C = 512
CODE_DEV = 2048
CLIPS = 2
TF_DEV = 2
ROWS_DEV = 2
WIDTH = 128
FRAMES = 4
HEIGHT = 32
CODES = 32768


def owner_codes(key, salt):
    key = jax.random.fold_in(key, salt)
    slab_count = FRAMES // TF_DEV
    band_count = HEIGHT // ROWS_DEV
    per_block = CLIPS * TF_DEV * ROWS_DEV * WIDTH
    capacity = 2 * per_block // band_count
    slot_total = band_count * capacity
    subkeys = jax.random.split(key, 5)
    heat_level = jax.random.randint(subkeys[0], (slab_count, band_count, band_count), 0, 3)
    hottest = jax.random.randint(subkeys[1], (slab_count,), 0, band_count)
    heat_level = jnp.where(jnp.arange(band_count)[None, None, :] == hottest[:, None, None], 4, heat_level)
    slot_owner = jnp.arange(slot_total) // capacity
    orders = jax.vmap(lambda subkey: jax.random.permutation(subkey, slot_total))(jax.random.split(subkeys[2], slab_count * band_count)).reshape(slab_count, band_count, slot_total)
    scores = heat_level[:, :, slot_owner] * slot_total + orders
    chosen = jnp.argsort(-scores, axis=-1, stable=True)[:, :, :per_block]
    owners = chosen // capacity
    shuffles = jax.vmap(lambda subkey: jax.random.permutation(subkey, per_block))(jax.random.split(subkeys[3], slab_count * band_count)).reshape(slab_count, band_count, per_block)
    owners = jnp.take_along_axis(owners, shuffles, axis=-1)
    within = jax.random.randint(subkeys[4], (slab_count, band_count, per_block), 0, CODE_DEV)
    codes = owners * CODE_DEV + within
    codes = codes.reshape(slab_count, band_count, CLIPS, TF_DEV, ROWS_DEV, WIDTH)
    codes = codes.transpose(2, 0, 3, 1, 4, 5).reshape(CLIPS, FRAMES, HEIGHT, WIDTH)
    return codes.astype(jnp.int32)


def draw_codes_first(key, part):
    return owner_codes(key, 11)


def draw_codes_second(key, part):
    return owner_codes(key, 23)


def shard_levels(stream_key, extent, cuts, low, high):
    level = 1.0
    for dim, parts in cuts:
        heights = jax.random.uniform(jax.random.fold_in(jax.random.fold_in(stream_key, 6), dim), (parts,), jnp.float32, low / len(cuts), high / len(cuts))
        level = level * jnp.repeat(jnp.exp(heights), extent[dim] // parts).reshape((-1,) + (1,) * (len(extent) - 1 - dim))
    return level


def centred(own_key, shape, spread, limit, pieces=(), dtype=jnp.bfloat16):
    level = shard_levels(own_key, shape, pieces, -0.22, 0.18) if pieces else 1.0
    values = jax.random.normal(own_key, shape, jnp.float32) * spread * level
    return jnp.minimum(jnp.maximum(values, -limit), limit).astype(dtype)


def setup_inputs(seed: int = 0) -> dict:
    arg_keys = jax.random.split(jax.random.key(seed), 11)
    return {
        "latents": centred(arg_keys[0], (CLIPS, FRAMES, HEIGHT, WIDTH, C), 1.0, 6.0, ((1, 2), (2, 16))),
        "norm_gain": jnp.clip(1.0 + 0.15 * jax.random.normal(arg_keys[1], (C,), jnp.float32), 0.25, 1.75),
        "spatial_weight": centred(arg_keys[2], (3, 3, C, C), (9 * C) ** -0.5, 0.09375),
        "temporal_weight": centred(arg_keys[3], (3, C), 0.6, 3.0, (), jnp.float32),
        "codebooks": centred(arg_keys[4], (2, CODES, C), 1.0, 6.0, ((1, 16),)),
        "ema_counts": jnp.clip(jnp.exp(math.log(30.0) - 4.6051701 * jax.random.uniform(arg_keys[5], (2, CODES), jnp.float32) ** shard_levels(arg_keys[5], (2, CODES), ((1, 16),), -0.2, 0.2)), 0.3, 30.0),
        "ema_sums": centred(arg_keys[6], (2, CODES, C), 1.0, 6.0, ((1, 16), (2, 2)), jnp.float32),
        "decay": jnp.clip(jax.random.uniform(arg_keys[7], (2,), jnp.float32, 0.6, 0.9), 0.6, 0.9),
        "codes_first": draw_codes_first(jax.random.fold_in(arg_keys[10], 71), 0),
        "codes_second": draw_codes_second(jax.random.fold_in(arg_keys[10], 71), 0),
    }


def reference(latents, norm_gain, spatial_weight, temporal_weight, codebooks, ema_counts, ema_sums, decay, codes_first, codes_second):
    widened = latents.astype(jnp.float32)
    inverse = lax.rsqrt(lax.optimization_barrier(jnp.mean(widened * widened, axis=-1, keepdims=True)) + 1e-06)
    normed = (widened * inverse * norm_gain).astype(jnp.bfloat16)
    frame_stack = normed.reshape(CLIPS * FRAMES, HEIGHT, WIDTH, C)

    def convolve(frame):
        padded = jnp.pad(frame, ((1, 1), (1, 1), (0, 0)))
        summed = jnp.zeros((HEIGHT * WIDTH, C), jnp.float32)
        for row_tap in range(3):
            for col_tap in range(3):
                window = padded[row_tap:row_tap + HEIGHT, col_tap:col_tap + WIDTH].reshape(-1, C)
                summed = summed + jnp.dot(window, spatial_weight[row_tap, col_tap], preferred_element_type=jnp.float32)
        return jax.nn.silu(summed).astype(jnp.bfloat16).reshape(HEIGHT, WIDTH, C)
    hidden = lax.map(convolve, frame_stack).reshape(CLIPS, FRAMES, HEIGHT, WIDTH, C)
    delayed = jnp.pad(hidden, ((0, 0), (2, 0), (0, 0), (0, 0), (0, 0)))
    mixed = jnp.zeros(latents.shape, jnp.float32)
    for tap in range(3):
        mixed = mixed + temporal_weight[tap] * delayed[:, tap:tap + FRAMES].astype(jnp.float32)
    encoded = (widened + mixed).astype(jnp.bfloat16)
    flat = encoded.reshape(-1, C)
    first_ids = codes_first.reshape(-1)
    second_ids = codes_second.reshape(-1)
    first_quant = jnp.take(codebooks[0], first_ids, axis=0)
    residual = (flat.astype(jnp.float32) - first_quant.astype(jnp.float32)).astype(jnp.bfloat16)
    second_quant = jnp.take(codebooks[1], second_ids, axis=0)
    leftover = residual.astype(jnp.float32) - second_quant.astype(jnp.float32)
    error = lax.optimization_barrier(jnp.mean(leftover * leftover, axis=-1)).reshape(codes_first.shape)
    unit = jnp.ones(first_ids.shape, jnp.float32)
    counts = jnp.stack([jax.ops.segment_sum(unit, first_ids, num_segments=CODES), jax.ops.segment_sum(unit, second_ids, num_segments=CODES)])
    sums = jnp.stack([jax.ops.segment_sum(flat.astype(jnp.float32), first_ids, num_segments=CODES), jax.ops.segment_sum(residual.astype(jnp.float32), second_ids, num_segments=CODES)])
    keep = decay[:, None]
    ema_counts_new = keep * ema_counts + (1.0 - keep) * counts
    ema_sums_new = decay[:, None, None] * ema_sums + (1.0 - decay[:, None, None]) * sums
    return (ema_counts_new, ema_sums_new, error)
```

```python
import jax
import jax.numpy as jnp
from jax import lax
from jax.sharding import PartitionSpec as P


def with_rows(x):
    peers, length = lax.axis_size("height"), x.shape[2]
    up = [(i, i + 1) for i in range(peers - 1)]
    down = [(j, i) for i, j in up]
    before = lax.ppermute(x[:, :, length - 1 :], "height", up)
    after = lax.ppermute(x[:, :, :1], "height", down)
    return jnp.concatenate([before, x, after], axis=2)


def normalize(values, norm_gain):
    widened = values.astype(jnp.float32)
    inverse = lax.rsqrt(jnp.mean(widened * widened, axis=-1, keepdims=True) + 1e-06)
    return (widened * inverse * norm_gain).astype(jnp.bfloat16)


def convolve(padded, kernel):
    clips, frames, rows, width, channels = padded.shape
    summed = lax.conv_general_dilated(
        padded.reshape(clips * frames, rows, width, channels),
        kernel,
        (1, 1),
        ((0, 0), (1, 1)),
        dimension_numbers=("NHWC", "HWIO", "NHWC"),
        preferred_element_type=jnp.float32,
    )
    hidden = jax.nn.silu(summed).astype(jnp.bfloat16)
    return hidden.reshape(clips, frames, rows - 2, width, channels)


def slots_of(indices, num_peers, capacity, code_rows):
    owners = indices // code_rows
    markers = (owners[:, None] == jnp.arange(num_peers, dtype=jnp.int32)[None, :]).astype(jnp.int32)
    ranking = jnp.sum((jnp.cumsum(markers, axis=0) - 1) * markers, axis=1)
    return owners * capacity + ranking


def wanted_of(indices, slot_ids, total):
    match = slot_ids[None, :] == jnp.arange(total, dtype=jnp.int32)[:, None]
    return jnp.sum(jnp.where(match, indices[None, :] + 1, 0), axis=1) - 1


def rows_by(ids, count):
    return (ids[:, None] == jnp.arange(count, dtype=jnp.int32)[None, :]).astype(jnp.bfloat16)


def picked(ids, table):
    return jnp.dot(
        rows_by(ids, table.shape[0]), table, preferred_element_type=jnp.float32
    ).astype(jnp.bfloat16)


def body(
    latents,
    norm_gain,
    spatial_weight,
    temporal_weight,
    codebooks,
    ema_counts,
    ema_sums,
    decay,
    codes_first,
    codes_second,
):
    frame_count = latents.shape[1]
    channels = latents.shape[-1]
    num_peers = lax.axis_size("height")
    slabs = lax.axis_size("tm")
    part = channels // slabs
    code_rows = codebooks.shape[1]
    amount = codes_first.size
    capacity = 2 * amount // num_peers
    total = num_peers * capacity
    offset = lax.axis_index("height") * code_rows
    slab = lax.axis_index("tm")
    everyone = ("tm", "height")

    slots = [
        slots_of(codes.reshape(-1), num_peers, capacity, code_rows)
        for codes in (codes_first, codes_second)
    ]
    wanted = jnp.stack(
        [
            wanted_of(codes.reshape(-1), slot, total).reshape(num_peers, capacity)
            for codes, slot in zip((codes_first, codes_second), slots)
        ],
        axis=1,
    )
    wanted = jnp.broadcast_to(wanted[None], (slabs,) + wanted.shape).reshape(
        slabs * num_peers, 2 * capacity
    )
    got = lax.all_to_all(wanted, everyone, split_axis=0, concat_axis=0, tiled=True)
    got = got.reshape(slabs, num_peers, 2, capacity) - offset
    mine = lax.dynamic_index_in_dim(got[:, :, 0], slab, 0, keepdims=False)
    answer = picked(mine.reshape(-1), codebooks[0]).reshape(num_peers, capacity, channels)
    answer = lax.all_to_all(answer, "height", split_axis=0, concat_axis=0, tiled=True)
    first_quant = picked(slots[0], answer.reshape(total, channels))

    widened = latents.astype(jnp.float32)
    normed = normalize(latents, norm_gain)
    hidden = convolve(with_rows(normed), spatial_weight)
    earlier = lax.ppermute(hidden, "tm", [(i, i + 1) for i in range(slabs - 1)])
    sequence = jnp.concatenate([earlier, hidden], axis=1)
    mixed = jnp.zeros(latents.shape, jnp.float32)
    for tap in range(3):
        begin = frame_count - 2 + tap
        mixed = mixed + temporal_weight[tap] * sequence[:, begin : begin + frame_count].astype(
            jnp.float32
        )
    encoded = (widened + mixed).astype(jnp.bfloat16)
    flat = encoded.reshape(-1, channels)

    def deliver(vectors, slot):
        packed = jnp.dot(
            (jnp.arange(total, dtype=jnp.int32)[:, None] == slot[None, :]).astype(jnp.bfloat16),
            vectors,
            preferred_element_type=jnp.float32,
        ).astype(jnp.bfloat16)
        packed = packed.reshape(num_peers, capacity, slabs, part).transpose(2, 0, 1, 3)
        packed = packed.reshape(slabs * num_peers, capacity, part)
        there = lax.all_to_all(packed, everyone, split_axis=0, concat_axis=0, tiled=True)
        return there.reshape(-1, part)

    def tally(ids, vectors):
        hot = jnp.arange(code_rows, dtype=jnp.int32)[:, None] == ids[None, :]
        sums = jnp.dot(hot.astype(jnp.bfloat16), vectors, preferred_element_type=jnp.float32)
        return (sums, jnp.sum(hot.astype(jnp.float32), axis=1))

    first_ids, second_ids = got[:, :, 0].reshape(-1), got[:, :, 1].reshape(-1)
    residual = (flat.astype(jnp.float32) - first_quant.astype(jnp.float32)).astype(jnp.bfloat16)
    first_there = deliver(flat, slots[0])
    second_there = deliver(residual, slots[1])

    table = lax.dynamic_slice_in_dim(codebooks[1], slab * part, part, axis=1)
    second_quant = picked(second_ids, table)
    leftover = second_there.astype(jnp.float32) - second_quant.astype(jnp.float32)
    squares = jnp.sum(leftover * leftover, axis=-1).reshape(slabs * num_peers, capacity)
    squares = lax.all_to_all(squares, everyone, split_axis=0, concat_axis=0, tiled=True)
    squares = jnp.sum(squares.reshape(slabs, total), axis=0)
    match = slots[1][:, None] == jnp.arange(total, dtype=jnp.int32)[None, :]
    error = jnp.sum(jnp.where(match, squares[None, :], 0.0), axis=1) / channels
    error = error.reshape(codes_first.shape)

    tallies = [tally(first_ids, first_there), tally(second_ids, second_there)]
    sums = jnp.stack([item[0] for item in tallies])
    counts = jnp.stack([item[1] for item in tallies])
    keep = decay[:, None]
    ema_counts_new = keep * ema_counts + (1.0 - keep) * counts
    ema_sums_new = decay[:, None, None] * ema_sums + (1.0 - decay[:, None, None]) * sums
    return (ema_counts_new, ema_sums_new, error)


def solution(mesh):
    return jax.shard_map(
        body,
        mesh=mesh,
        in_specs=(
            P(None, "tm", "height", None, None),
            P(),
            P(),
            P(),
            P(None, "height", None),
            P(None, "height"),
            P(None, "height", "tm"),
            P(),
            P(None, "tm", "height", None),
            P(None, "tm", "height", None),
        ),
        out_specs=(P(None, "height"), P(None, "height", "tm"), P(None, "tm", "height", None)),
        check_vma=False,
    )
```

```python
import jax
import jax.numpy as jnp
from jax import lax
from jax.experimental import pallas as pl
from jax.experimental.pallas import tpu as pltpu
from jax.sharding import PartitionSpec as P


def normalize(values, norm_gain):
    widened = values.astype(jnp.float32)
    inverse = lax.rsqrt(jnp.mean(widened * widened, axis=-1, keepdims=True) + 1e-06)
    return (widened * inverse * norm_gain).astype(jnp.bfloat16)


def convolve(padded, kernel):
    clips, frames, rows, width, channels = padded.shape
    summed = lax.conv_general_dilated(
        padded.reshape(clips * frames, rows, width, channels),
        kernel,
        (1, 1),
        ((0, 0), (1, 1)),
        dimension_numbers=("NHWC", "HWIO", "NHWC"),
        preferred_element_type=jnp.float32,
    )
    hidden = jax.nn.silu(summed).astype(jnp.bfloat16)
    return hidden.reshape(clips, frames, rows - 2, width, channels)


def slots_of(indices, num_peers, capacity, code_rows):
    amount = indices.shape[1]
    owners = indices // code_rows
    markers = (owners[:, :, None] == jnp.arange(num_peers, dtype=jnp.int32)).astype(jnp.bfloat16)
    steps = jnp.arange(amount, dtype=jnp.int32)
    earlier = (steps[:, None] > steps[None, :]).astype(jnp.bfloat16)
    before = jnp.einsum("ij,sjp->isp", earlier, markers, preferred_element_type=jnp.float32)
    ranking = jnp.sum(before.swapaxes(0, 1) * markers.astype(jnp.float32), axis=2)
    return owners * capacity + ranking.astype(jnp.int32)


def wanted_of(indices, slot_ids, total):
    match = slot_ids[:, None, :] == jnp.arange(total, dtype=jnp.int32)[None, :, None]
    return jnp.sum(jnp.where(match, indices[:, None, :] + 1, 0), axis=2) - 1


def block_of(count, limit):
    block = count
    while block > limit and block % 2 == 0:
        block //= 2
    return block


def pack(slot_ids, vectors, total, slabs):
    amount, channels = vectors.shape
    part = channels // slabs
    block = block_of(total, 512)

    def kernel(slot_ref, vector_ref, out_ref):
        start = pl.program_id(0) * block
        places = start + lax.broadcasted_iota(jnp.int32, (block, amount), 0)
        hot = jnp.where(places == slot_ref[...], 1.0, 0.0).astype(jnp.bfloat16)
        rows = jnp.dot(hot, vector_ref[...], preferred_element_type=jnp.float32)
        rows = rows.astype(jnp.bfloat16)
        for slab in range(slabs):
            out_ref[slab] = rows[:, slab * part : (slab + 1) * part]

    return pl.pallas_call(
        kernel,
        grid=(total // block,),
        out_shape=jax.ShapeDtypeStruct((slabs, total, part), jnp.bfloat16),
        in_specs=[
            pl.BlockSpec((1, amount), lambda i: (0, 0)),
            pl.BlockSpec((amount, channels), lambda i: (0, 0)),
        ],
        out_specs=pl.BlockSpec((slabs, block, part), lambda i: (0, i, 0)),
        cost_estimate=pl.CostEstimate(
            flops=2 * total * amount * channels, bytes_accessed=6 * total * part * slabs, transcendentals=0
        ),
        name="pack",
    )(slot_ids[None, :], vectors)


def tally(which, ids, vectors, ema_sums, decay, into):
    amount, part = vectors.shape
    code_rows = ema_sums.shape[1]
    block = block_of(code_rows, 256)

    def kernel(decay_ref, id_ref, vector_ref, old_ref, *rest):
        out_ref = rest[-1]
        start = pl.program_id(0) * block
        places = start + lax.broadcasted_iota(jnp.int32, (block, amount), 0)
        hot = jnp.where(places == id_ref[...], 1.0, 0.0).astype(jnp.bfloat16)
        sums = jnp.dot(hot, vector_ref[...], preferred_element_type=jnp.float32)
        keep = decay_ref[which]
        out_ref[0] = keep * old_ref[0] + (1.0 - keep) * sums

    operands = [decay, ids[None, :], vectors, ema_sums]
    in_specs = [
        pl.BlockSpec(memory_space=pltpu.SMEM),
        pl.BlockSpec((1, amount), lambda i: (0, 0)),
        pl.BlockSpec((amount, part), lambda i: (0, 0)),
        pl.BlockSpec((1, block, part), lambda i: (which, i, 0)),
    ]
    aliases = {}
    if into is not None:
        operands.append(into)
        in_specs.append(pl.BlockSpec(memory_space=pl.ANY))
        aliases = {4: 0}
    return pl.pallas_call(
        kernel,
        grid=(code_rows // block,),
        out_shape=jax.ShapeDtypeStruct(ema_sums.shape, jnp.float32),
        in_specs=in_specs,
        out_specs=pl.BlockSpec((1, block, part), lambda i: (which, i, 0)),
        input_output_aliases=aliases,
        cost_estimate=pl.CostEstimate(
            flops=2 * code_rows * amount * part, bytes_accessed=8 * code_rows * part, transcendentals=0
        ),
        name="tally",
    )(*operands)


def rows_by(ids, count):
    return (ids[:, None] == jnp.arange(count, dtype=jnp.int32)[None, :]).astype(jnp.bfloat16)


def picked(ids, table):
    return jnp.dot(
        rows_by(ids, table.shape[0]), table, preferred_element_type=jnp.float32
    ).astype(jnp.bfloat16)


def body(
    latents,
    norm_gain,
    spatial_weight,
    temporal_weight,
    codebooks,
    ema_counts,
    ema_sums,
    decay,
    codes_first,
    codes_second,
):
    frame_count = latents.shape[1]
    channels = latents.shape[-1]
    num_peers = lax.axis_size("height")
    slabs = lax.axis_size("tm")
    part = channels // slabs
    code_rows = codebooks.shape[1]
    amount = codes_first.size
    capacity = 2 * amount // num_peers
    total = num_peers * capacity
    offset = lax.axis_index("height") * code_rows
    slab = lax.axis_index("tm")
    everyone = ("tm", "height")

    peers = [(i, i + 1) for i in range(num_peers - 1)]
    first_row = normalize(latents[:, :, :1], norm_gain)
    last_row = normalize(latents[:, :, -1:], norm_gain)
    codes = jnp.stack([codes_first.reshape(-1), codes_second.reshape(-1)])
    first_row, last_row, codes = lax.optimization_barrier((first_row, last_row, codes))
    row_before = lax.ppermute(last_row, "height", peers)
    row_after = lax.ppermute(first_row, "height", [(j, i) for i, j in peers])

    slots = slots_of(codes, num_peers, capacity, code_rows)
    wanted = wanted_of(codes, slots, total).reshape(2, num_peers, capacity).swapaxes(0, 1)
    wanted = jnp.broadcast_to(wanted[None], (slabs,) + wanted.shape).reshape(
        slabs * num_peers, 2 * capacity
    )
    got = lax.all_to_all(wanted, everyone, split_axis=0, concat_axis=0, tiled=True)
    got = got.reshape(slabs, num_peers, 2, capacity) - offset
    mine = lax.dynamic_index_in_dim(got[:, :, 0], slab, 0, keepdims=False)
    answer = picked(mine.reshape(-1), codebooks[0]).reshape(num_peers, capacity, channels)
    answer = lax.all_to_all(answer, "height", split_axis=0, concat_axis=0, tiled=True)

    widened = latents.astype(jnp.float32)
    normed = normalize(latents, norm_gain)
    padded = jnp.concatenate([row_before, normed, row_after], axis=2)
    hidden = convolve(padded, spatial_weight)
    earlier = lax.ppermute(hidden, "tm", [(i, i + 1) for i in range(slabs - 1)])
    first_ids, second_ids = got[:, :, 0].reshape(-1), got[:, :, 1].reshape(-1)
    table = lax.dynamic_slice_in_dim(codebooks[1], slab * part, part, axis=1)
    second_quant = picked(second_ids, table)
    marks = jnp.arange(code_rows, dtype=jnp.int32)[:, None]
    counts = jnp.stack(
        [
            jnp.sum((marks == ids[None, :]).astype(jnp.float32), axis=1)
            for ids in (first_ids, second_ids)
        ]
    )
    earlier, second_quant = lax.optimization_barrier((earlier, second_quant))
    sequence = jnp.concatenate([earlier, hidden], axis=1)
    mixed = jnp.zeros(latents.shape, jnp.float32)
    for tap in range(3):
        begin = frame_count - 2 + tap
        mixed = mixed + temporal_weight[tap] * sequence[:, begin : begin + frame_count].astype(
            jnp.float32
        )
    encoded = (widened + mixed).astype(jnp.bfloat16)
    flat = encoded.reshape(-1, channels)

    def deliver(vectors, slot):
        packed = pack(slot, vectors, total, slabs).reshape(slabs * num_peers, capacity, part)
        there = lax.all_to_all(packed, everyone, split_axis=0, concat_axis=0, tiled=True)
        return there.reshape(-1, part)

    first_there = deliver(flat, slots[0])
    first_quant = picked(slots[0], answer.reshape(total, channels))
    residual = (flat.astype(jnp.float32) - first_quant.astype(jnp.float32)).astype(jnp.bfloat16)
    second_there = deliver(residual, slots[1])

    leftover = second_there.astype(jnp.float32) - second_quant.astype(jnp.float32)
    squares = jnp.sum(leftover * leftover, axis=-1).reshape(slabs * num_peers, capacity)
    squares = lax.all_to_all(squares, everyone, split_axis=0, concat_axis=0, tiled=True)
    squares = jnp.sum(squares.reshape(slabs, total), axis=0)
    match = slots[1][:, None] == jnp.arange(total, dtype=jnp.int32)[None, :]
    error = jnp.sum(jnp.where(match, squares[None, :], 0.0), axis=1) / channels
    error = error.reshape(codes_first.shape)

    ema_sums_new = tally(0, first_ids, first_there, ema_sums, decay, None)
    ema_sums_new = tally(1, second_ids, second_there, ema_sums, decay, ema_sums_new)
    keep = decay[:, None]
    ema_counts_new = keep * ema_counts + (1.0 - keep) * counts
    return (ema_counts_new, ema_sums_new, error)


def solution(mesh):
    return jax.shard_map(
        body,
        mesh=mesh,
        in_specs=(
            P(None, "tm", "height", None, None),
            P(),
            P(),
            P(),
            P(None, "height", None),
            P(None, "height"),
            P(None, "height", "tm"),
            P(),
            P(None, "tm", "height", None),
            P(None, "tm", "height", None),
        ),
        out_specs=(P(None, "height"), P(None, "height", "tm"), P(None, "tm", "height", None)),
        check_vma=False,
    )
```

```python
import jax
import jax.numpy as jnp
from jax import lax
from jax.experimental import pallas as pl
from jax.experimental.pallas import tpu as pltpu
from jax.sharding import PartitionSpec as P


def normalize(values, norm_gain):
    widened = values.astype(jnp.float32)
    inverse = lax.rsqrt(jnp.mean(widened * widened, axis=-1, keepdims=True) + 1e-06)
    return (widened * inverse * norm_gain).astype(jnp.bfloat16)


def convolve(padded, kernel):
    clips, frames, rows, width, channels = padded.shape
    summed = lax.conv_general_dilated(
        padded.reshape(clips * frames, rows, width, channels),
        kernel,
        (1, 1),
        ((0, 0), (1, 1)),
        dimension_numbers=("NHWC", "HWIO", "NHWC"),
        preferred_element_type=jnp.float32,
    )
    hidden = jax.nn.silu(summed).astype(jnp.bfloat16)
    return hidden.reshape(clips, frames, rows - 2, width, channels)


def slots_of(indices, num_peers, capacity, code_rows):
    amount = indices.shape[1]
    owners = indices // code_rows
    markers = (owners[:, :, None] == jnp.arange(num_peers, dtype=jnp.int32)).astype(jnp.bfloat16)
    steps = jnp.arange(amount, dtype=jnp.int32)
    earlier = (steps[:, None] > steps[None, :]).astype(jnp.bfloat16)
    before = jnp.einsum("ij,sjp->isp", earlier, markers, preferred_element_type=jnp.float32)
    ranking = jnp.sum(before.swapaxes(0, 1) * markers.astype(jnp.float32), axis=2)
    return owners * capacity + ranking.astype(jnp.int32)


def wanted_of(indices, slot_ids, total):
    match = slot_ids[:, None, :] == jnp.arange(total, dtype=jnp.int32)[None, :, None]
    return jnp.sum(jnp.where(match, indices[:, None, :] + 1, 0), axis=2) - 1


def block_of(count, limit):
    block = count
    while block > limit and block % 2 == 0:
        block //= 2
    return block


def pack(slot_ids, vectors, total, slabs):
    amount, channels = vectors.shape
    part = channels // slabs
    block = block_of(total, 512)

    def kernel(slot_ref, vector_ref, out_ref):
        start = pl.program_id(0) * block
        places = start + lax.broadcasted_iota(jnp.int32, (block, amount), 0)
        hot = jnp.where(places == slot_ref[...], 1.0, 0.0).astype(jnp.bfloat16)
        rows = jnp.dot(hot, vector_ref[...], preferred_element_type=jnp.float32)
        rows = rows.astype(jnp.bfloat16)
        for slab in range(slabs):
            out_ref[slab] = rows[:, slab * part : (slab + 1) * part]

    return pl.pallas_call(
        kernel,
        grid=(total // block,),
        out_shape=jax.ShapeDtypeStruct((slabs, total, part), jnp.bfloat16),
        in_specs=[
            pl.BlockSpec((1, amount), lambda i: (0, 0)),
            pl.BlockSpec((amount, channels), lambda i: (0, 0)),
        ],
        out_specs=pl.BlockSpec((slabs, block, part), lambda i: (0, i, 0)),
        cost_estimate=pl.CostEstimate(
            flops=2 * total * amount * channels, bytes_accessed=6 * total * part * slabs, transcendentals=0
        ),
        name="pack",
    )(slot_ids[None, :], vectors)


def exchange(first, second, first_ids, second_ids, second_quant, ema_sums, decay, slabs, num_peers):
    members, capacity, part = first.shape
    code_rows = ema_sums.shape[1]
    amount = members * capacity
    block = code_rows
    while block * amount > 2**20 and block % 2 == 0:
        block //= 2
    blocks = code_rows // block

    def kernel(
        first_ref,
        second_ref,
        first_id_ref,
        second_id_ref,
        quant_ref,
        old_ref,
        decay_ref,
        sums_ref,
        error_ref,
        first_in,
        second_in,
        squares,
        local_sems,
        send_sems,
        recv_sems,
    ):
        me_slab = lax.axis_index("tm")
        me_row = lax.axis_index("height")
        me = me_slab * num_peers + me_row

        def peer_of(step):
            peer = lax.rem(me + step, members)
            return peer, {"tm": peer // num_peers, "height": lax.rem(peer, num_peers)}

        barrier = pltpu.get_barrier_semaphore()

        @pl.loop(1, members)
        def _(step):
            _, target = peer_of(step)
            pl.semaphore_signal(
                barrier, inc=1, device_id=target, device_id_type=pl.DeviceIdType.MESH
            )

        pl.semaphore_wait(barrier, members - 1)

        def send(source, landing, which):
            @pl.loop(1, members)
            def _(step):
                peer, target = peer_of(step)
                pltpu.make_async_remote_copy(
                    src_ref=source.at[peer],
                    dst_ref=landing.at[me],
                    send_sem=send_sems.at[which],
                    recv_sem=recv_sems.at[which],
                    device_id=target,
                    device_id_type=pl.DeviceIdType.MESH,
                ).start()

        def own(source, landing, which):
            return pltpu.make_async_copy(source.at[me], landing.at[me], local_sems.at[which])

        def finish(landing, sems, which):
            most = landing.at[pl.ds(0, members - 1)]
            pltpu.make_async_copy(most, most, sems.at[which]).wait()

        send(first_ref, first_in, 0)
        send(second_ref, second_in, 1)
        own(first_ref, first_in, 0).start()
        own(second_ref, second_in, 1).start()

        def tally(which, id_ref, landing, begin, end):
            ids = id_ref[...]
            keep = decay_ref[which]

            @pl.loop(begin, end)
            def _(step):
                start = pl.multiple_of(step * block, block)
                places = start + lax.broadcasted_iota(jnp.int32, (block, amount), 0)
                hot = jnp.where(places == ids, 1.0, 0.0).astype(jnp.bfloat16)
                vectors = landing[...].reshape(amount, part)
                sums = jnp.dot(hot, vectors, preferred_element_type=jnp.float32)
                here = pl.ds(start, block)
                sums_ref[which, here, :] = keep * old_ref[which, here, :] + (1.0 - keep) * sums

        own(first_ref, first_in, 0).wait()
        finish(first_in, recv_sems, 0)
        tally(0, first_id_ref, first_in, 0, blocks)
        own(second_ref, second_in, 1).wait()
        finish(second_in, recv_sems, 1)

        @pl.loop(0, members)
        def _(source):
            leftover = second_in[source].astype(jnp.float32) - quant_ref[source].astype(jnp.float32)
            squares[source] = jnp.sum(leftover * leftover, axis=1)[None, :]

        tally(1, second_id_ref, second_in, 0, 1)
        send(squares, error_ref, 2)
        own(squares, error_ref, 2).start()
        tally(1, second_id_ref, second_in, 1, blocks)
        own(squares, error_ref, 2).wait()
        finish(error_ref, recv_sems, 2)
        finish(first_in, send_sems, 0)
        finish(second_in, send_sems, 1)
        finish(error_ref, send_sems, 2)

    vmem = pl.BlockSpec(memory_space=pltpu.VMEM)
    return pl.pallas_call(
        kernel,
        out_shape=(
            jax.ShapeDtypeStruct(ema_sums.shape, jnp.float32),
            jax.ShapeDtypeStruct((members, 1, capacity), jnp.float32),
        ),
        in_specs=[vmem] * 6 + [pl.BlockSpec(memory_space=pltpu.SMEM)],
        out_specs=(vmem, vmem),
        scratch_shapes=[
            pltpu.VMEM(first.shape, jnp.bfloat16),
            pltpu.VMEM(second.shape, jnp.bfloat16),
            pltpu.VMEM((members, 1, capacity), jnp.float32),
            pltpu.SemaphoreType.DMA((3,)),
            pltpu.SemaphoreType.DMA((3,)),
            pltpu.SemaphoreType.DMA((3,)),
        ],
        compiler_params=pltpu.CompilerParams(
            collective_id=0, has_side_effects=True, vmem_limit_bytes=60 * 2**20
        ),
        name="exchange",
    )(
        first,
        second,
        first_ids[None, :],
        second_ids[None, :],
        second_quant.reshape(members, capacity, part),
        ema_sums,
        decay,
    )


def rows_by(ids, count):
    return (ids[:, None] == jnp.arange(count, dtype=jnp.int32)[None, :]).astype(jnp.bfloat16)


def picked(ids, table):
    return jnp.dot(
        rows_by(ids, table.shape[0]), table, preferred_element_type=jnp.float32
    ).astype(jnp.bfloat16)


def body(
    latents,
    norm_gain,
    spatial_weight,
    temporal_weight,
    codebooks,
    ema_counts,
    ema_sums,
    decay,
    codes_first,
    codes_second,
):
    frame_count = latents.shape[1]
    channels = latents.shape[-1]
    num_peers = lax.axis_size("height")
    slabs = lax.axis_size("tm")
    part = channels // slabs
    code_rows = codebooks.shape[1]
    amount = codes_first.size
    capacity = 2 * amount // num_peers
    total = num_peers * capacity
    offset = lax.axis_index("height") * code_rows
    slab = lax.axis_index("tm")
    everyone = ("tm", "height")

    peers = [(i, i + 1) for i in range(num_peers - 1)]
    first_row = normalize(latents[:, :, :1], norm_gain)
    last_row = normalize(latents[:, :, -1:], norm_gain)
    codes = jnp.stack([codes_first.reshape(-1), codes_second.reshape(-1)])
    first_row, last_row, codes = lax.optimization_barrier((first_row, last_row, codes))
    row_before = lax.ppermute(last_row, "height", peers)
    row_after = lax.ppermute(first_row, "height", [(j, i) for i, j in peers])

    slots = slots_of(codes, num_peers, capacity, code_rows)
    wanted = wanted_of(codes, slots, total).reshape(2, num_peers, capacity).swapaxes(0, 1)
    wanted = jnp.broadcast_to(wanted[None], (slabs,) + wanted.shape).reshape(
        slabs * num_peers, 2 * capacity
    )
    got = lax.all_to_all(wanted, everyone, split_axis=0, concat_axis=0, tiled=True)
    got = got.reshape(slabs, num_peers, 2, capacity) - offset
    mine = lax.dynamic_index_in_dim(got[:, :, 0], slab, 0, keepdims=False)
    answer = picked(mine.reshape(-1), codebooks[0]).reshape(num_peers, capacity, channels)
    answer = lax.all_to_all(answer, "height", split_axis=0, concat_axis=0, tiled=True)

    widened = latents.astype(jnp.float32)
    normed = normalize(latents, norm_gain)
    padded = jnp.concatenate([row_before, normed, row_after], axis=2)
    hidden = convolve(padded, spatial_weight)
    earlier = lax.ppermute(hidden, "tm", [(i, i + 1) for i in range(slabs - 1)])
    first_ids, second_ids = got[:, :, 0].reshape(-1), got[:, :, 1].reshape(-1)
    table = lax.dynamic_slice_in_dim(codebooks[1], slab * part, part, axis=1)
    second_quant = picked(second_ids, table)
    marks = jnp.arange(code_rows, dtype=jnp.int32)[:, None]
    counts = jnp.stack(
        [
            jnp.sum((marks == ids[None, :]).astype(jnp.float32), axis=1)
            for ids in (first_ids, second_ids)
        ]
    )
    earlier, second_quant = lax.optimization_barrier((earlier, second_quant))
    sequence = jnp.concatenate([earlier, hidden], axis=1)
    mixed = jnp.zeros(latents.shape, jnp.float32)
    for tap in range(3):
        begin = frame_count - 2 + tap
        mixed = mixed + temporal_weight[tap] * sequence[:, begin : begin + frame_count].astype(
            jnp.float32
        )
    encoded = (widened + mixed).astype(jnp.bfloat16)
    flat = encoded.reshape(-1, channels)

    def packed(vectors, slot):
        return pack(slot, vectors, total, slabs).reshape(slabs * num_peers, capacity, part)

    first_quant = picked(slots[0], answer.reshape(total, channels))
    residual = (flat.astype(jnp.float32) - first_quant.astype(jnp.float32)).astype(jnp.bfloat16)
    ema_sums_new, squares = exchange(
        packed(flat, slots[0]),
        packed(residual, slots[1]),
        first_ids,
        second_ids,
        second_quant,
        ema_sums,
        decay,
        slabs,
        num_peers,
    )
    squares = jnp.sum(squares.reshape(slabs, total), axis=0)
    match = slots[1][:, None] == jnp.arange(total, dtype=jnp.int32)[None, :]
    error = jnp.sum(jnp.where(match, squares[None, :], 0.0), axis=1) / channels
    error = error.reshape(codes_first.shape)

    keep = decay[:, None]
    ema_counts_new = keep * ema_counts + (1.0 - keep) * counts
    return (ema_counts_new, ema_sums_new, error)


def solution(mesh):
    return jax.shard_map(
        body,
        mesh=mesh,
        in_specs=(
            P(None, "tm", "height", None, None),
            P(),
            P(),
            P(),
            P(None, "height", None),
            P(None, "height"),
            P(None, "height", "tm"),
            P(),
            P(None, "tm", "height", None),
            P(None, "tm", "height", None),
        ),
        out_specs=(P(None, "height"), P(None, "height", "tm"), P(None, "tm", "height", None)),
        check_vma=False,
    )
```

```python
import jax
import jax.numpy as jnp
from jax import lax
from jax.experimental import pallas as pl
from jax.experimental.pallas import tpu as pltpu
from jax.sharding import PartitionSpec as P


def normalize(values, norm_gain):
    widened = values.astype(jnp.float32)
    inverse = lax.rsqrt(jnp.mean(widened * widened, axis=-1, keepdims=True) + 1e-06)
    return (widened * inverse * norm_gain).astype(jnp.bfloat16)


def convolve(latents, norm_gain, row_before, row_after, kernel):
    clips, frames, rows, width, channels = latents.shape
    images = clips * frames

    def body(latent_ref, gain_ref, before_ref, after_ref, weight_ref, out_ref):
        normed = normalize(latent_ref[0].reshape(rows * width, channels), gain_ref[...])
        taps = jnp.concatenate([before_ref[0], normed, after_ref[0]], axis=0)
        windows = [taps[row * width : (row + rows) * width] for row in range(3)]
        column = lax.broadcasted_iota(jnp.int32, (rows * width, channels), 0) % width

        def tap(col):
            total = jnp.dot(windows[0], weight_ref[0, col], preferred_element_type=jnp.float32)
            for row in (1, 2):
                total += jnp.dot(
                    windows[row], weight_ref[row, col], preferred_element_type=jnp.float32
                )
            return total

        summed = tap(1)
        summed += jnp.where(column == 0, 0.0, pltpu.roll(tap(0), 1, 0))
        summed += jnp.where(column == width - 1, 0.0, pltpu.roll(tap(2), rows * width - 1, 0))
        hidden = jax.nn.silu(summed).astype(jnp.bfloat16)
        out_ref[0] = hidden.reshape(rows, width, channels)

    hidden = pl.pallas_call(
        body,
        grid=(images,),
        out_shape=jax.ShapeDtypeStruct((images, rows, width, channels), jnp.bfloat16),
        in_specs=[
            pl.BlockSpec((1, rows, width, channels), lambda i: (i, 0, 0, 0)),
            pl.BlockSpec((1, channels), lambda i: (0, 0)),
            pl.BlockSpec((1, width, channels), lambda i: (i, 0, 0)),
            pl.BlockSpec((1, width, channels), lambda i: (i, 0, 0)),
            pl.BlockSpec(kernel.shape, lambda i: (0, 0, 0, 0)),
        ],
        out_specs=pl.BlockSpec((1, rows, width, channels), lambda i: (i, 0, 0, 0)),
        compiler_params=pltpu.CompilerParams(vmem_limit_bytes=40 * 2**20),
        cost_estimate=pl.CostEstimate(
            flops=18 * images * rows * width * channels * channels,
            bytes_accessed=2 * kernel.size + 4 * latents.size,
            transcendentals=latents.size,
        ),
        name="convolve",
    )(
        latents.reshape(images, rows, width, channels),
        norm_gain[None, :],
        row_before.reshape(images, width, channels),
        row_after.reshape(images, width, channels),
        kernel,
    )
    return hidden.reshape(latents.shape)


def ask(codes, num_peers, slabs, capacity, code_rows):
    amount = codes.shape[1]
    members = slabs * num_peers
    total = num_peers * capacity

    def kernel(code_ref, slot_ref, ids_ref, outgoing, local_sem, send_sem, recv_sem):
        me_row = lax.axis_index("height")
        me = lax.axis_index("tm") * num_peers + me_row

        def peer_of(step):
            peer = lax.rem(me + step, members)
            row = lax.rem(peer, num_peers)
            return row, {"tm": peer // num_peers, "height": row}

        barrier = pltpu.get_barrier_semaphore()

        @pl.loop(1, members)
        def _(step):
            _, target = peer_of(step)
            pl.semaphore_signal(
                barrier, inc=1, device_id=target, device_id_type=pl.DeviceIdType.MESH
            )

        owners = lax.broadcasted_iota(jnp.int32, (num_peers, amount), 0)
        later = lax.broadcasted_iota(jnp.int32, (amount, amount), 1)
        sooner = lax.broadcasted_iota(jnp.int32, (amount, amount), 0)
        order = jnp.where(sooner < later, 1.0, 0.0).astype(jnp.bfloat16)
        for which in range(2):
            code = code_ref[which : which + 1, :]
            local = code - owners * code_rows
            mark = jnp.where((local >= 0) & (local < code_rows), 1.0, 0.0)
            before = jnp.dot(
                mark.astype(jnp.bfloat16), order, preferred_element_type=jnp.float32
            )
            place = mark * (before + (owners * capacity).astype(jnp.float32))
            slot = jnp.sum(place, axis=0, keepdims=True)
            local = jnp.sum(jnp.where(mark > 0.0, local, 0), axis=0, keepdims=True)
            slot_ref[which : which + 1, :] = slot.astype(jnp.int32)
            high = (local // 256).astype(jnp.float32)
            low = (local % 256).astype(jnp.float32)
            kind = lax.broadcasted_iota(jnp.int32, (16, amount), 0)
            digits = jnp.where(kind == 0, high, jnp.where(kind == 1, low, 1.0))
            digits = digits.astype(jnp.bfloat16)
            places = lax.broadcasted_iota(jnp.int32, (total, amount), 0).astype(jnp.float32)
            hot = jnp.where(places == slot, 1.0, 0.0).astype(jnp.bfloat16)
            found = lax.dot_general(
                digits, hot, (((1,), (1,)), ((), ())), preferred_element_type=jnp.float32
            )
            wanted = found[0:1] * 256.0 + found[1:2] + found[2:3] - 1.0
            wanted = wanted.astype(jnp.int32)
            for row in range(num_peers):
                outgoing[row, which : which + 1, :] = wanted[
                    :, row * capacity : (row + 1) * capacity
                ]

        pl.semaphore_wait(barrier, members - 1)

        @pl.loop(1, members)
        def _(step):
            row, target = peer_of(step)
            pltpu.make_async_remote_copy(
                src_ref=outgoing.at[row],
                dst_ref=ids_ref.at[me],
                send_sem=send_sem,
                recv_sem=recv_sem,
                device_id=target,
                device_id_type=pl.DeviceIdType.MESH,
            ).start()

        own = pltpu.make_async_copy(outgoing.at[me_row], ids_ref.at[me], local_sem)
        own.start()
        own.wait()
        most = ids_ref.at[pl.ds(0, members - 1)]
        pltpu.make_async_copy(most, most, recv_sem).wait()
        pltpu.make_async_copy(most, most, send_sem).wait()

    vmem = pl.BlockSpec(memory_space=pltpu.VMEM)
    return pl.pallas_call(
        kernel,
        out_shape=(
            jax.ShapeDtypeStruct(codes.shape, jnp.int32),
            jax.ShapeDtypeStruct((members, 2, capacity), jnp.int32),
        ),
        in_specs=[vmem],
        out_specs=(vmem, vmem),
        scratch_shapes=[
            pltpu.VMEM((num_peers, 2, capacity), jnp.int32),
            pltpu.SemaphoreType.DMA,
            pltpu.SemaphoreType.DMA,
            pltpu.SemaphoreType.DMA,
        ],
        compiler_params=pltpu.CompilerParams(
            collective_id=1, has_side_effects=True, vmem_limit_bytes=60 * 2**20
        ),
        name="ask",
    )(codes)


def block_of(count, limit):
    block = count
    while block > limit and block % 2 == 0:
        block //= 2
    return block


def pack(slot_ids, vectors, total, slabs):
    amount, channels = vectors.shape
    part = channels // slabs
    block = block_of(total, 512)

    def kernel(slot_ref, vector_ref, out_ref):
        start = pl.program_id(0) * block
        places = start + lax.broadcasted_iota(jnp.int32, (block, amount), 0)
        hot = jnp.where(places == slot_ref[...], 1.0, 0.0).astype(jnp.bfloat16)
        rows = jnp.dot(hot, vector_ref[...], preferred_element_type=jnp.float32)
        rows = rows.astype(jnp.bfloat16)
        for slab in range(slabs):
            out_ref[slab] = rows[:, slab * part : (slab + 1) * part]

    return pl.pallas_call(
        kernel,
        grid=(total // block,),
        out_shape=jax.ShapeDtypeStruct((slabs, total, part), jnp.bfloat16),
        in_specs=[
            pl.BlockSpec((1, amount), lambda i: (0, 0)),
            pl.BlockSpec((amount, channels), lambda i: (0, 0)),
        ],
        out_specs=pl.BlockSpec((slabs, block, part), lambda i: (0, i, 0)),
        cost_estimate=pl.CostEstimate(
            flops=2 * total * amount * channels, bytes_accessed=6 * total * part * slabs, transcendentals=0
        ),
        name="pack",
    )(slot_ids[None, :], vectors)


def exchange(first, flat, answer, slots, first_ids, second_ids, second_quant, ema_sums, decay, slabs, num_peers):
    members, capacity, part = first.shape
    tokens, channels = flat.shape
    total = num_peers * capacity
    pick_block, pack_block = block_of(tokens, 256), capacity * block_of(num_peers, 4)
    code_rows = ema_sums.shape[1]
    amount = members * capacity
    block = code_rows
    while block * amount > 2**20 and block % 2 == 0:
        block //= 2
    blocks = code_rows // block

    def kernel(
        first_ref,
        flat_ref,
        answer_ref,
        place_ref,
        slot_ref,
        first_id_ref,
        second_id_ref,
        quant_ref,
        old_ref,
        decay_ref,
        sums_ref,
        error_ref,
        residual,
        second_out,
        first_in,
        second_in,
        squares,
        local_sems,
        send_sems,
        recv_sems,
    ):
        me_slab = lax.axis_index("tm")
        me_row = lax.axis_index("height")
        me = me_slab * num_peers + me_row

        def peer_of(step):
            peer = lax.rem(me + step, members)
            return peer, {"tm": peer // num_peers, "height": lax.rem(peer, num_peers)}

        barrier = pltpu.get_barrier_semaphore()

        @pl.loop(1, members)
        def _(step):
            _, target = peer_of(step)
            pl.semaphore_signal(
                barrier, inc=1, device_id=target, device_id_type=pl.DeviceIdType.MESH
            )

        pl.semaphore_wait(barrier, members - 1)

        def send(source, landing, which):
            @pl.loop(1, members)
            def _(step):
                peer, target = peer_of(step)
                pltpu.make_async_remote_copy(
                    src_ref=source.at[peer],
                    dst_ref=landing.at[me],
                    send_sem=send_sems.at[which],
                    recv_sem=recv_sems.at[which],
                    device_id=target,
                    device_id_type=pl.DeviceIdType.MESH,
                ).start()

        def own(source, landing, which):
            return pltpu.make_async_copy(source.at[me], landing.at[me], local_sems.at[which])

        def finish(landing, sems, which):
            most = landing.at[pl.ds(0, members - 1)]
            pltpu.make_async_copy(most, most, sems.at[which]).wait()

        send(first_ref, first_in, 0)
        own(first_ref, first_in, 0).start()

        @pl.loop(0, tokens // pick_block)
        def _(step):
            here = pl.ds(pl.multiple_of(step * pick_block, pick_block), pick_block)
            places = lax.broadcasted_iota(jnp.int32, (pick_block, total), 1)
            hot = jnp.where(places == place_ref[here, :], 1.0, 0.0).astype(jnp.bfloat16)
            quant = jnp.dot(hot, answer_ref[...], preferred_element_type=jnp.float32)
            residual[here, :] = (flat_ref[here, :].astype(jnp.float32) - quant).astype(jnp.bfloat16)

        @pl.loop(0, total // pack_block)
        def _(step):
            places = step * pack_block + lax.broadcasted_iota(jnp.int32, (pack_block, tokens), 0)
            hot = jnp.where(places == slot_ref[...], 1.0, 0.0).astype(jnp.bfloat16)
            rows = jnp.dot(hot, residual[...], preferred_element_type=jnp.float32)
            rows = rows.astype(jnp.bfloat16)
            count = pack_block // capacity
            for slab in range(slabs):
                second_out[pl.ds(slab * num_peers + step * count, count)] = rows[
                    :, slab * part : (slab + 1) * part
                ].reshape(count, capacity, part)

        send(second_out, second_in, 1)
        own(second_out, second_in, 1).start()

        def tally(which, id_ref, landing, begin, end):
            ids = id_ref[...]
            keep = decay_ref[which]

            @pl.loop(begin, end)
            def _(step):
                start = pl.multiple_of(step * block, block)
                places = start + lax.broadcasted_iota(jnp.int32, (block, amount), 0)
                hot = jnp.where(places == ids, 1.0, 0.0).astype(jnp.bfloat16)
                vectors = landing[...].reshape(amount, part)
                sums = jnp.dot(hot, vectors, preferred_element_type=jnp.float32)
                here = pl.ds(start, block)
                sums_ref[which, here, :] = keep * old_ref[which, here, :] + (1.0 - keep) * sums

        own(first_ref, first_in, 0).wait()
        finish(first_in, recv_sems, 0)
        tally(0, first_id_ref, first_in, 0, blocks)
        own(second_out, second_in, 1).wait()
        finish(second_in, recv_sems, 1)

        @pl.loop(0, members)
        def _(source):
            leftover = second_in[source].astype(jnp.float32) - quant_ref[source].astype(jnp.float32)
            squares[source] = jnp.sum(leftover * leftover, axis=1)[None, :]

        tally(1, second_id_ref, second_in, 0, 1)
        send(squares, error_ref, 2)
        own(squares, error_ref, 2).start()
        tally(1, second_id_ref, second_in, 1, blocks)
        own(squares, error_ref, 2).wait()
        finish(error_ref, recv_sems, 2)
        finish(first_in, send_sems, 0)
        finish(second_in, send_sems, 1)
        finish(error_ref, send_sems, 2)

    vmem = pl.BlockSpec(memory_space=pltpu.VMEM)
    return pl.pallas_call(
        kernel,
        out_shape=(
            jax.ShapeDtypeStruct(ema_sums.shape, jnp.float32),
            jax.ShapeDtypeStruct((members, 1, capacity), jnp.float32),
        ),
        in_specs=[vmem] * 9 + [pl.BlockSpec(memory_space=pltpu.SMEM)],
        out_specs=(vmem, vmem),
        scratch_shapes=[
            pltpu.VMEM(flat.shape, jnp.bfloat16),
            pltpu.VMEM(first.shape, jnp.bfloat16),
            pltpu.VMEM(first.shape, jnp.bfloat16),
            pltpu.VMEM(first.shape, jnp.bfloat16),
            pltpu.VMEM((members, 1, capacity), jnp.float32),
            pltpu.SemaphoreType.DMA((3,)),
            pltpu.SemaphoreType.DMA((3,)),
            pltpu.SemaphoreType.DMA((3,)),
        ],
        compiler_params=pltpu.CompilerParams(
            collective_id=0, has_side_effects=True, vmem_limit_bytes=60 * 2**20
        ),
        name="exchange",
    )(
        first,
        flat,
        answer,
        slots[0][:, None],
        slots[1][None, :],
        first_ids[None, :],
        second_ids[None, :],
        second_quant.reshape(members, capacity, part),
        ema_sums,
        decay,
    )


def rows_by(ids, count):
    return (ids[:, None] == jnp.arange(count, dtype=jnp.int32)[None, :]).astype(jnp.bfloat16)


def picked(ids, table):
    return jnp.dot(
        rows_by(ids, table.shape[0]), table, preferred_element_type=jnp.float32
    ).astype(jnp.bfloat16)


def body(
    latents,
    norm_gain,
    spatial_weight,
    temporal_weight,
    codebooks,
    ema_counts,
    ema_sums,
    decay,
    codes_first,
    codes_second,
):
    frame_count = latents.shape[1]
    channels = latents.shape[-1]
    num_peers = lax.axis_size("height")
    slabs = lax.axis_size("tm")
    part = channels // slabs
    code_rows = codebooks.shape[1]
    amount = codes_first.size
    capacity = 2 * amount // num_peers
    total = num_peers * capacity
    slab = lax.axis_index("tm")
    everyone = ("tm", "height")

    peers = [(i, i + 1) for i in range(num_peers - 1)]
    first_row = normalize(latents[:, :, :1], norm_gain)
    last_row = normalize(latents[:, :, -1:], norm_gain)
    codes = jnp.stack([codes_first.reshape(-1), codes_second.reshape(-1)])
    first_row, last_row, codes = lax.optimization_barrier((first_row, last_row, codes))
    row_before = lax.ppermute(last_row, "height", peers)
    row_after = lax.ppermute(first_row, "height", [(j, i) for i, j in peers])

    slots, got = ask(codes, num_peers, slabs, capacity, code_rows)
    got = got.reshape(slabs, num_peers, 2, capacity)
    mine = lax.dynamic_index_in_dim(got[:, :, 0], slab, 0, keepdims=False)
    answer = picked(mine.reshape(-1), codebooks[0]).reshape(num_peers, capacity, channels)
    answer = lax.all_to_all(answer, "height", split_axis=0, concat_axis=0, tiled=True)

    widened = latents.astype(jnp.float32)
    hidden = convolve(latents, norm_gain, row_before, row_after, spatial_weight)
    earlier = lax.ppermute(hidden, "tm", [(i, i + 1) for i in range(slabs - 1)])
    first_ids, second_ids = got[:, :, 0].reshape(-1), got[:, :, 1].reshape(-1)
    table = lax.dynamic_slice_in_dim(codebooks[1], slab * part, part, axis=1)
    second_quant = picked(second_ids, table)
    marks = jnp.arange(code_rows, dtype=jnp.int32)[:, None]
    counts = jnp.stack(
        [
            jnp.sum((marks == ids[None, :]).astype(jnp.float32), axis=1)
            for ids in (first_ids, second_ids)
        ]
    )
    earlier, second_quant = lax.optimization_barrier((earlier, second_quant))
    sequence = jnp.concatenate([earlier, hidden], axis=1)
    mixed = jnp.zeros(latents.shape, jnp.float32)
    for tap in range(3):
        begin = frame_count - 2 + tap
        mixed = mixed + temporal_weight[tap] * sequence[:, begin : begin + frame_count].astype(
            jnp.float32
        )
    encoded = (widened + mixed).astype(jnp.bfloat16)
    flat = encoded.reshape(-1, channels)

    packed = pack(slots[0], flat, total, slabs).reshape(slabs * num_peers, capacity, part)
    ema_sums_new, squares = exchange(
        packed,
        flat,
        answer.reshape(total, channels),
        slots,
        first_ids,
        second_ids,
        second_quant,
        ema_sums,
        decay,
        slabs,
        num_peers,
    )
    squares = jnp.sum(squares.reshape(slabs, total), axis=0)
    match = slots[1][:, None] == jnp.arange(total, dtype=jnp.int32)[None, :]
    error = jnp.sum(jnp.where(match, squares[None, :], 0.0), axis=1) / channels
    error = error.reshape(codes_first.shape)

    keep = decay[:, None]
    ema_counts_new = keep * ema_counts + (1.0 - keep) * counts
    return (ema_counts_new, ema_sums_new, error)


def solution(mesh):
    return jax.shard_map(
        body,
        mesh=mesh,
        in_specs=(
            P(None, "tm", "height", None, None),
            P(),
            P(),
            P(),
            P(None, "height", None),
            P(None, "height"),
            P(None, "height", "tm"),
            P(),
            P(None, "tm", "height", None),
            P(None, "tm", "height", None),
        ),
        out_specs=(P(None, "height"), P(None, "height", "tm"), P(None, "tm", "height", None)),
        check_vma=False,
    )
```

```python
import jax
import jax.numpy as jnp
from jax import lax
from jax.experimental import pallas as pl
from jax.experimental.pallas import tpu as pltpu
from jax.sharding import PartitionSpec as P


def normalize(values, norm_gain):
    widened = values.astype(jnp.float32)
    inverse = lax.rsqrt(jnp.mean(widened * widened, axis=-1, keepdims=True) + 1e-06)
    return (widened * inverse * norm_gain).astype(jnp.bfloat16)


def ask(codes, num_peers, slabs, capacity, code_rows):
    amount = codes.shape[1]
    members = slabs * num_peers
    total = num_peers * capacity

    def kernel(code_ref, slot_ref, ids_ref, outgoing, local_sem, send_sem, recv_sem):
        me_row = lax.axis_index("height")
        me = lax.axis_index("tm") * num_peers + me_row

        def peer_of(step):
            peer = lax.rem(me + step, members)
            row = lax.rem(peer, num_peers)
            return row, {"tm": peer // num_peers, "height": row}

        barrier = pltpu.get_barrier_semaphore()

        @pl.loop(1, members)
        def _(step):
            _, target = peer_of(step)
            pl.semaphore_signal(
                barrier, inc=1, device_id=target, device_id_type=pl.DeviceIdType.MESH
            )

        owners = lax.broadcasted_iota(jnp.int32, (num_peers, amount), 0)
        later = lax.broadcasted_iota(jnp.int32, (amount, amount), 1)
        sooner = lax.broadcasted_iota(jnp.int32, (amount, amount), 0)
        order = jnp.where(sooner < later, 1.0, 0.0).astype(jnp.bfloat16)
        for which in range(2):
            code = code_ref[which : which + 1, :]
            local = code - owners * code_rows
            mark = jnp.where((local >= 0) & (local < code_rows), 1.0, 0.0)
            before = jnp.dot(
                mark.astype(jnp.bfloat16), order, preferred_element_type=jnp.float32
            )
            place = mark * (before + (owners * capacity).astype(jnp.float32))
            slot = jnp.sum(place, axis=0, keepdims=True)
            local = jnp.sum(jnp.where(mark > 0.0, local, 0), axis=0, keepdims=True)
            slot_ref[which : which + 1, :] = slot.astype(jnp.int32)
            high = (local // 256).astype(jnp.float32)
            low = (local % 256).astype(jnp.float32)
            kind = lax.broadcasted_iota(jnp.int32, (16, amount), 0)
            digits = jnp.where(kind == 0, high, jnp.where(kind == 1, low, 1.0))
            digits = digits.astype(jnp.bfloat16)
            places = lax.broadcasted_iota(jnp.int32, (total, amount), 0).astype(jnp.float32)
            hot = jnp.where(places == slot, 1.0, 0.0).astype(jnp.bfloat16)
            found = lax.dot_general(
                digits, hot, (((1,), (1,)), ((), ())), preferred_element_type=jnp.float32
            )
            wanted = found[0:1] * 256.0 + found[1:2] + found[2:3] - 1.0
            wanted = wanted.astype(jnp.int32)
            for row in range(num_peers):
                outgoing[row, which : which + 1, :] = wanted[
                    :, row * capacity : (row + 1) * capacity
                ]

        pl.semaphore_wait(barrier, members - 1)

        @pl.loop(1, members)
        def _(step):
            row, target = peer_of(step)
            pltpu.make_async_remote_copy(
                src_ref=outgoing.at[row],
                dst_ref=ids_ref.at[me],
                send_sem=send_sem,
                recv_sem=recv_sem,
                device_id=target,
                device_id_type=pl.DeviceIdType.MESH,
            ).start()

        own = pltpu.make_async_copy(outgoing.at[me_row], ids_ref.at[me], local_sem)
        own.start()
        own.wait()
        most = ids_ref.at[pl.ds(0, members - 1)]
        pltpu.make_async_copy(most, most, recv_sem).wait()
        pltpu.make_async_copy(most, most, send_sem).wait()

    vmem = pl.BlockSpec(memory_space=pltpu.VMEM)
    return pl.pallas_call(
        kernel,
        out_shape=(
            jax.ShapeDtypeStruct(codes.shape, jnp.int32),
            jax.ShapeDtypeStruct((members, 2, capacity), jnp.int32),
        ),
        in_specs=[vmem],
        out_specs=(vmem, vmem),
        scratch_shapes=[
            pltpu.VMEM((num_peers, 2, capacity), jnp.int32),
            pltpu.SemaphoreType.DMA,
            pltpu.SemaphoreType.DMA,
            pltpu.SemaphoreType.DMA,
        ],
        compiler_params=pltpu.CompilerParams(
            collective_id=1, has_side_effects=True, vmem_limit_bytes=60 * 2**20
        ),
        name="ask",
    )(codes)


def block_of(count, limit):
    block = count
    while block > limit and block % 2 == 0:
        block //= 2
    return block


def main(
    latents,
    norm_gain,
    row_before,
    row_after,
    spatial_weight,
    temporal_weight,
    codebooks,
    table,
    got,
    slots,
    slabs,
    num_peers,
    capacity,
):
    clips, frames, rows, width, channels = latents.shape
    images, pixels = clips * frames, rows * width
    tokens = images * pixels
    part = channels // slabs
    members, total = slabs * num_peers, num_peers * capacity
    amount = members * capacity
    code_rows = codebooks.shape[1]
    group = block_of(num_peers, 4)
    span = group * capacity
    pick_block = block_of(tokens, 256)
    block = code_rows
    while block * amount > 2**20 and block % 2 == 0:
        block //= 2
    blocks = code_rows // block

    def kernel(
        latent_ref,
        gain_ref,
        before_ref,
        after_ref,
        temporal_ref,
        table_ref,
        first_id_ref,
        second_id_ref,
        first_slot_ref,
        second_slot_ref,
        weight_hbm,
        book_hbm,
        sums_ref,
        error_ref,
        count_ref,
        weight_ref,
        book_ref,
        served,
        answer,
        hidden,
        earlier,
        flat,
        residual,
        first_out,
        second_out,
        first_in,
        second_in,
        quants,
        squares,
        load_sems,
        local_sems,
        send_sems,
        recv_sems,
    ):
        me_slab = lax.axis_index("tm")
        me_row = lax.axis_index("height")
        me = me_slab * num_peers + me_row
        load_book = pltpu.make_async_copy(book_hbm.at[0], book_ref, load_sems.at[0])
        load_weight = pltpu.make_async_copy(weight_hbm, weight_ref, load_sems.at[1])
        load_book.start()
        load_weight.start()

        def peer_of(step):
            peer = lax.rem(me + step, members)
            return peer, {"tm": peer // num_peers, "height": lax.rem(peer, num_peers)}

        def push(source, landing, which, target):
            return pltpu.make_async_remote_copy(
                src_ref=source,
                dst_ref=landing,
                send_sem=send_sems.at[which],
                recv_sem=recv_sems.at[which],
                device_id=target,
                device_id_type=pl.DeviceIdType.MESH,
            )

        def send(source, landing, which):
            @pl.loop(1, members)
            def _(step):
                peer, target = peer_of(step)
                push(source.at[peer], landing.at[me], which, target).start()

        def own(source, landing, which, at):
            return pltpu.make_async_copy(source.at[at], landing.at[at], local_sems.at[which])

        def rows_at(ids, table):
            marks = lax.broadcasted_iota(jnp.int32, (table.shape[0], ids.shape[1]), 0)
            hot = jnp.where(marks == ids, 1.0, 0.0).astype(jnp.bfloat16)
            return lax.dot_general(
                hot, table, (((0,), (0,)), ((), ())), preferred_element_type=jnp.float32
            )

        def finish(landing, sems, which, count):
            most = landing.at[pl.ds(0, count)]
            pltpu.make_async_copy(most, most, sems.at[which]).wait()

        barrier = pltpu.get_barrier_semaphore()

        @pl.loop(1, members)
        def _(step):
            _, target = peer_of(step)
            pl.semaphore_signal(
                barrier, inc=1, device_id=target, device_id_type=pl.DeviceIdType.MESH
            )

        load_book.wait()
        pl.semaphore_wait(barrier, members - 1)

        @pl.loop(0, num_peers // group)
        def _(step):
            base = lax.rem(me_row // group + step, num_peers // group) * group
            here = pl.ds(pl.multiple_of(me_slab * total + base * capacity, span), span)
            found = rows_at(first_id_ref[:, here], book_ref[...])
            found = found.astype(jnp.bfloat16).reshape(group, capacity, channels)
            served[pl.ds(base, group)] = found

            @pl.loop(0, group)
            def _(offset):
                peer = base + offset

                @pl.when(peer != me_row)
                def _():
                    target = {"tm": me_slab, "height": peer}
                    push(served.at[peer], answer.at[me_row], 3, target).start()

        own(served, answer, 3, me_row).start()
        load_weight.wait()
        last_slab = me_slab + 1 >= slabs
        column = lax.rem(lax.broadcasted_iota(jnp.int32, (pixels, channels), 0), width)

        def forward(image):
            return push(
                hidden.at[image],
                earlier.at[image],
                4,
                {"tm": lax.rem(me_slab + 1, slabs), "height": me_row},
            )

        @pl.loop(0, images)
        def _(image):
            normed = normalize(latent_ref[image], gain_ref[...])
            taps = jnp.concatenate([before_ref[image], normed, after_ref[image]], axis=0)
            windows = [taps[row * width : (row + rows) * width] for row in range(3)]

            def tap(col):
                added = jnp.dot(windows[0], weight_ref[0, col], preferred_element_type=jnp.float32)
                for row in (1, 2):
                    added += jnp.dot(
                        windows[row], weight_ref[row, col], preferred_element_type=jnp.float32
                    )
                return added

            summed = tap(1)
            summed += jnp.where(column == 0, 0.0, pltpu.roll(tap(0), 1, 0))
            summed += jnp.where(column == width - 1, 0.0, pltpu.roll(tap(2), pixels - 1, 0))
            hidden[image] = (summed / (1.0 + jnp.exp(-summed))).astype(jnp.bfloat16)

            @pl.when(jnp.logical_not(last_slab))
            def _():
                forward(image).start()

        @pl.loop(0, members // group)
        def _(step):
            here = pl.ds(pl.multiple_of(step * span, span), span)
            found = rows_at(second_id_ref[:, here], table_ref[...])
            found = found.astype(jnp.bfloat16).reshape(group, capacity, part)
            quants[pl.ds(step * group, group)] = found

        @pl.when(me_slab > 0)
        def _():
            finish(earlier, recv_sems, 4, images)

        @pl.when(me_slab == 0)
        def _():
            earlier[...] = jnp.zeros(earlier.shape, jnp.bfloat16)

        for image in range(images):
            clip, frame = image // frames, image % frames
            mixed = jnp.zeros((pixels, channels), jnp.float32)
            for tap in range(3):
                at = frame - 2 + tap
                frame_ref = hidden if at >= 0 else earlier
                value = frame_ref[clip * frames + at % frames].astype(jnp.float32)
                mixed = mixed + temporal_ref[tap : tap + 1, :] * value
            encoded = latent_ref[image].astype(jnp.float32) + mixed
            flat[image * pixels : (image + 1) * pixels, :] = encoded.astype(jnp.bfloat16)

        def pack(slot_ref, vectors, out):
            @pl.loop(0, num_peers // group)
            def _(step):
                places = step * span + lax.broadcasted_iota(jnp.int32, (span, tokens), 0)
                hot = jnp.where(places == slot_ref[...], 1.0, 0.0).astype(jnp.bfloat16)
                packed = jnp.dot(hot, vectors[...], preferred_element_type=jnp.float32)
                packed = packed.astype(jnp.bfloat16)
                for slab in range(slabs):
                    out[pl.ds(slab * num_peers + step * group, group)] = packed[
                        :, slab * part : (slab + 1) * part
                    ].reshape(group, capacity, part)

        pack(first_slot_ref, flat, first_out)
        send(first_out, first_in, 0)
        own(first_out, first_in, 0, me).start()
        own(served, answer, 3, me_row).wait()
        finish(answer, recv_sems, 3, num_peers - 1)

        @pl.loop(0, tokens // pick_block)
        def _(step):
            here = pl.ds(pl.multiple_of(step * pick_block, pick_block), pick_block)
            quant = rows_at(first_slot_ref[:, here], answer[...].reshape(total, channels))
            residual[here, :] = (flat[here, :].astype(jnp.float32) - quant).astype(jnp.bfloat16)

        pack(second_slot_ref, residual, second_out)
        send(second_out, second_in, 1)
        own(second_out, second_in, 1, me).start()

        def tally(which, id_ref, landing, begin, end):
            ids = id_ref[...]

            @pl.loop(begin, end)
            def _(step):
                start = pl.multiple_of(step * block, block)
                places = start + lax.broadcasted_iota(jnp.int32, (block, amount), 0)
                hot = jnp.where(places == ids, 1.0, 0.0).astype(jnp.bfloat16)
                vectors = landing[...].reshape(amount, part)
                sums_ref[which, pl.ds(start, block), :] = jnp.dot(
                    hot, vectors, preferred_element_type=jnp.float32
                )

        for which, id_ref in ((0, first_id_ref), (1, second_id_ref)):
            ids = id_ref[...]

            @pl.loop(0, blocks)
            def _(step):
                marks = step * block + lax.broadcasted_iota(jnp.int32, (block, amount), 0)
                hot = jnp.where(marks == ids, 1.0, 0.0)
                count_ref[which, step] = jnp.sum(hot, axis=1)[None, :]

        own(first_out, first_in, 0, me).wait()
        finish(first_in, recv_sems, 0, members - 1)
        tally(0, first_id_ref, first_in, 0, blocks)
        own(second_out, second_in, 1, me).wait()
        finish(second_in, recv_sems, 1, members - 1)

        @pl.loop(0, members)
        def _(source):
            leftover = second_in[source].astype(jnp.float32) - quants[source].astype(jnp.float32)
            squares[source] = jnp.sum(leftover * leftover, axis=1)[None, :]

        tally(1, second_id_ref, second_in, 0, 1)
        send(squares, error_ref, 2)
        own(squares, error_ref, 2, me).start()
        tally(1, second_id_ref, second_in, 1, blocks)
        own(squares, error_ref, 2, me).wait()
        finish(error_ref, recv_sems, 2, members - 1)
        finish(first_in, send_sems, 0, members - 1)
        finish(second_in, send_sems, 1, members - 1)
        finish(error_ref, send_sems, 2, members - 1)
        finish(answer, send_sems, 3, num_peers - 1)

        @pl.when(jnp.logical_not(last_slab))
        def _():
            finish(hidden, send_sems, 4, images)

    vmem, anywhere = pl.BlockSpec(memory_space=pltpu.VMEM), pl.BlockSpec(memory_space=pl.ANY)
    bf16 = jnp.bfloat16
    pieces = (members, capacity, part)
    first_ids, second_ids = got[:, 0].reshape(-1), got[:, 1].reshape(-1)
    return pl.pallas_call(
        kernel,
        out_shape=(
            jax.ShapeDtypeStruct((2, code_rows, part), jnp.float32),
            jax.ShapeDtypeStruct((members, 1, capacity), jnp.float32),
            jax.ShapeDtypeStruct((2, blocks, 1, block), jnp.float32),
        ),
        in_specs=[vmem] * 10 + [anywhere] * 2,
        out_specs=(vmem, vmem, vmem),
        scratch_shapes=[
            pltpu.VMEM(spatial_weight.shape, bf16),
            pltpu.VMEM((code_rows, channels), bf16),
            pltpu.VMEM((num_peers, capacity, channels), bf16),
            pltpu.VMEM((num_peers, capacity, channels), bf16),
            pltpu.VMEM((images, pixels, channels), bf16),
            pltpu.VMEM((images, pixels, channels), bf16),
            pltpu.VMEM((tokens, channels), bf16),
            pltpu.VMEM((tokens, channels), bf16),
            pltpu.VMEM(pieces, bf16),
            pltpu.VMEM(pieces, bf16),
            pltpu.VMEM(pieces, bf16),
            pltpu.VMEM(pieces, bf16),
            pltpu.VMEM(pieces, bf16),
            pltpu.VMEM((members, 1, capacity), jnp.float32),
            pltpu.SemaphoreType.DMA((2,)),
            pltpu.SemaphoreType.DMA((4,)),
            pltpu.SemaphoreType.DMA((5,)),
            pltpu.SemaphoreType.DMA((5,)),
        ],
        compiler_params=pltpu.CompilerParams(
            collective_id=0, has_side_effects=True, vmem_limit_bytes=60 * 2**20
        ),
        name="main",
    )(
        latents.reshape(images, pixels, channels),
        norm_gain[None, :],
        row_before.reshape(images, width, channels),
        row_after.reshape(images, width, channels),
        temporal_weight,
        table,
        first_ids[None, :],
        second_ids[None, :],
        slots[0][None, :],
        slots[1][None, :],
        spatial_weight,
        codebooks,
    )


def body(
    latents,
    norm_gain,
    spatial_weight,
    temporal_weight,
    codebooks,
    ema_counts,
    ema_sums,
    decay,
    codes_first,
    codes_second,
):
    channels = latents.shape[-1]
    num_peers = lax.axis_size("height")
    slabs = lax.axis_size("tm")
    part = channels // slabs
    code_rows = codebooks.shape[1]
    amount = codes_first.size
    capacity = 2 * amount // num_peers
    total = num_peers * capacity

    peers = [(i, i + 1) for i in range(num_peers - 1)]
    first_row = normalize(latents[:, :, :1], norm_gain)
    last_row = normalize(latents[:, :, -1:], norm_gain)
    codes = jnp.stack([codes_first.reshape(-1), codes_second.reshape(-1)])
    first_row, last_row, codes = lax.optimization_barrier((first_row, last_row, codes))
    row_before = lax.ppermute(last_row, "height", peers)
    row_after = lax.ppermute(first_row, "height", [(j, i) for i, j in peers])

    slots, got = ask(codes, num_peers, slabs, capacity, code_rows)
    table = lax.dynamic_slice_in_dim(codebooks[1], lax.axis_index("tm") * part, part, axis=1)
    sums, squares, counts = main(
        latents,
        norm_gain,
        row_before,
        row_after,
        spatial_weight,
        temporal_weight,
        codebooks,
        table,
        got,
        slots,
        slabs,
        num_peers,
        capacity,
    )
    squares = jnp.sum(squares.reshape(slabs, total), axis=0)
    match = slots[1][:, None] == jnp.arange(total, dtype=jnp.int32)[None, :]
    error = jnp.sum(jnp.where(match, squares[None, :], 0.0), axis=1) / channels
    error = error.reshape(codes_first.shape)

    counts = counts.reshape(2, code_rows)
    keep = decay[:, None]
    wide = decay[:, None, None]
    ema_sums_new = wide * ema_sums + (1.0 - wide) * sums
    ema_counts_new = keep * ema_counts + (1.0 - keep) * counts
    return (ema_counts_new, ema_sums_new, error)


def solution(mesh):
    return jax.shard_map(
        body,
        mesh=mesh,
        in_specs=(
            P(None, "tm", "height", None, None),
            P(),
            P(),
            P(),
            P(None, "height", None),
            P(None, "height"),
            P(None, "height", "tm"),
            P(),
            P(None, "tm", "height", None),
            P(None, "tm", "height", None),
        ),
        out_specs=(P(None, "height"), P(None, "height", "tm"), P(None, "tm", "height", None)),
        check_vma=False,
    )
```

```python
import jax
import jax.numpy as jnp
from jax import lax
from jax.experimental import pallas as pl
from jax.experimental.pallas import tpu as pltpu
from jax.sharding import PartitionSpec as P


def normalize(values, norm_gain):
    widened = values.astype(jnp.float32)
    inverse = lax.rsqrt(jnp.mean(widened * widened, axis=-1, keepdims=True) + 1e-06)
    return (widened * inverse * norm_gain).astype(jnp.bfloat16)


def ask(codes, num_peers, slabs, capacity, code_rows):
    amount = codes.shape[1]
    members = slabs * num_peers
    total = num_peers * capacity

    def kernel(code_ref, slot_ref, ids_ref, outgoing, local_sem, send_sem, recv_sem):
        me_row = lax.axis_index("height")
        me = lax.axis_index("tm") * num_peers + me_row

        def peer_of(step):
            peer = lax.rem(me + step, members)
            row = lax.rem(peer, num_peers)
            return row, {"tm": peer // num_peers, "height": row}

        barrier = pltpu.get_barrier_semaphore()

        @pl.loop(1, members)
        def _(step):
            _, target = peer_of(step)
            pl.semaphore_signal(
                barrier, inc=1, device_id=target, device_id_type=pl.DeviceIdType.MESH
            )

        owners = lax.broadcasted_iota(jnp.int32, (num_peers, amount), 0)
        later = lax.broadcasted_iota(jnp.int32, (amount, amount), 1)
        sooner = lax.broadcasted_iota(jnp.int32, (amount, amount), 0)
        order = jnp.where(sooner < later, 1.0, 0.0).astype(jnp.bfloat16)
        for which in range(2):
            code = code_ref[which : which + 1, :]
            local = code - owners * code_rows
            mark = jnp.where((local >= 0) & (local < code_rows), 1.0, 0.0)
            before = jnp.dot(
                mark.astype(jnp.bfloat16), order, preferred_element_type=jnp.float32
            )
            place = mark * (before + (owners * capacity).astype(jnp.float32))
            slot = jnp.sum(place, axis=0, keepdims=True)
            local = jnp.sum(jnp.where(mark > 0.0, local, 0), axis=0, keepdims=True)
            slot_ref[which : which + 1, :] = slot.astype(jnp.int32)
            high = (local // 256).astype(jnp.float32)
            low = (local % 256).astype(jnp.float32)
            kind = lax.broadcasted_iota(jnp.int32, (16, amount), 0)
            digits = jnp.where(kind == 0, high, jnp.where(kind == 1, low, 1.0))
            digits = digits.astype(jnp.bfloat16)
            places = lax.broadcasted_iota(jnp.int32, (total, amount), 0).astype(jnp.float32)
            hot = jnp.where(places == slot, 1.0, 0.0).astype(jnp.bfloat16)
            found = lax.dot_general(
                digits, hot, (((1,), (1,)), ((), ())), preferred_element_type=jnp.float32
            )
            wanted = found[0:1] * 256.0 + found[1:2] + found[2:3] - 1.0
            wanted = wanted.astype(jnp.int32)
            for row in range(num_peers):
                outgoing[row, which : which + 1, :] = wanted[
                    :, row * capacity : (row + 1) * capacity
                ]

        pl.semaphore_wait(barrier, members - 1)

        @pl.loop(1, members)
        def _(step):
            row, target = peer_of(step)
            pltpu.make_async_remote_copy(
                src_ref=outgoing.at[row],
                dst_ref=ids_ref.at[me],
                send_sem=send_sem,
                recv_sem=recv_sem,
                device_id=target,
                device_id_type=pl.DeviceIdType.MESH,
            ).start()

        own = pltpu.make_async_copy(outgoing.at[me_row], ids_ref.at[me], local_sem)
        own.start()
        own.wait()
        most = ids_ref.at[pl.ds(0, members - 1)]
        pltpu.make_async_copy(most, most, recv_sem).wait()
        pltpu.make_async_copy(most, most, send_sem).wait()

    vmem = pl.BlockSpec(memory_space=pltpu.VMEM)
    return pl.pallas_call(
        kernel,
        out_shape=(
            jax.ShapeDtypeStruct(codes.shape, jnp.int32),
            jax.ShapeDtypeStruct((members, 2, capacity), jnp.int32),
        ),
        in_specs=[vmem],
        out_specs=(vmem, vmem),
        scratch_shapes=[
            pltpu.VMEM((num_peers, 2, capacity), jnp.int32),
            pltpu.SemaphoreType.DMA,
            pltpu.SemaphoreType.DMA,
            pltpu.SemaphoreType.DMA,
        ],
        compiler_params=pltpu.CompilerParams(
            collective_id=1, has_side_effects=True, vmem_limit_bytes=60 * 2**20
        ),
        name="ask",
    )(codes)


def block_of(count, limit):
    block = count
    while block > limit and block % 2 == 0:
        block //= 2
    return block


def main(
    latents,
    norm_gain,
    spatial_weight,
    temporal_weight,
    codebooks,
    got,
    slots,
    slabs,
    num_peers,
    capacity,
):
    clips, frames, rows, width, channels = latents.shape
    images, pixels = clips * frames, rows * width
    tokens = images * pixels
    part = channels // slabs
    members, total = slabs * num_peers, num_peers * capacity
    amount = members * capacity
    code_rows = codebooks.shape[1]
    group = block_of(num_peers, 4)
    span = group * capacity
    pick_block = block_of(tokens, 256)
    block = code_rows
    while block * amount > 2**20 and block % 2 == 0:
        block //= 2
    blocks = code_rows // block

    def kernel(
        latent_ref,
        gain_ref,
        temporal_ref,
        first_id_ref,
        second_id_ref,
        first_slot_ref,
        second_slot_ref,
        weight_hbm,
        book_hbm,
        table_hbm,
        sums_ref,
        error_ref,
        count_ref,
        weight_ref,
        book_ref,
        table_ref,
        before_ref,
        after_ref,
        served,
        answer,
        hidden,
        earlier,
        flat,
        residual,
        first_out,
        second_out,
        first_in,
        second_in,
        quants,
        squares,
        load_sems,
        local_sems,
        send_sems,
        recv_sems,
    ):
        me_slab = lax.axis_index("tm")
        me_row = lax.axis_index("height")
        me = me_slab * num_peers + me_row
        load_book = pltpu.make_async_copy(book_hbm.at[0], book_ref, load_sems.at[0])
        load_weight = pltpu.make_async_copy(weight_hbm, weight_ref, load_sems.at[1])
        wanted = table_hbm
        if whole_table:
            lanes = pl.ds(pl.multiple_of(me_slab * part, part), part)
            wanted = table_hbm.at[1, :, lanes]
        load_table = pltpu.make_async_copy(wanted, table_ref, load_sems.at[2])
        load_book.start()
        load_weight.start()
        load_table.start()

        def peer_of(step):
            peer = lax.rem(me + step, members)
            return peer, {"tm": peer // num_peers, "height": lax.rem(peer, num_peers)}

        def push(source, landing, which, target):
            return pltpu.make_async_remote_copy(
                src_ref=source,
                dst_ref=landing,
                send_sem=send_sems.at[which],
                recv_sem=recv_sems.at[which],
                device_id=target,
                device_id_type=pl.DeviceIdType.MESH,
            )

        def send(source, landing, which):
            @pl.loop(1, members)
            def _(step):
                peer, target = peer_of(step)
                push(source.at[peer], landing.at[me], which, target).start()

        def own(source, landing, which, at):
            return pltpu.make_async_copy(source.at[at], landing.at[at], local_sems.at[which])

        def rows_at(ids, table):
            marks = lax.broadcasted_iota(jnp.int32, (table.shape[0], ids.shape[1]), 0)
            hot = jnp.where(marks == ids, 1.0, 0.0).astype(jnp.bfloat16)
            return lax.dot_general(
                hot, table, (((0,), (0,)), ((), ())), preferred_element_type=jnp.float32
            )

        def finish(landing, sems, which, count):
            most = landing.at[pl.ds(0, count)]
            pltpu.make_async_copy(most, most, sems.at[which]).wait()

        barrier = pltpu.get_barrier_semaphore()

        @pl.loop(1, members)
        def _(step):
            _, target = peer_of(step)
            pl.semaphore_signal(
                barrier, inc=1, device_id=target, device_id_type=pl.DeviceIdType.MESH
            )

        @pl.when(me_row == 0)
        def _():
            before_ref[...] = jnp.zeros(before_ref.shape, jnp.bfloat16)

        @pl.when(me_row == num_peers - 1)
        def _():
            after_ref[...] = jnp.zeros(after_ref.shape, jnp.bfloat16)

        pl.semaphore_wait(barrier, members - 1)

        def down():
            target = {"tm": me_slab, "height": lax.rem(me_row + 1, num_peers)}
            return push(latent_ref.at[:, pl.ds(pixels - width, width)], before_ref, 5, target)

        def up():
            target = {"tm": me_slab, "height": lax.rem(me_row + num_peers - 1, num_peers)}
            return push(latent_ref.at[:, pl.ds(0, width)], after_ref, 6, target)

        @pl.when(me_row < num_peers - 1)
        def _():
            down().start()

        @pl.when(me_row > 0)
        def _():
            up().start()

        load_book.wait()

        @pl.loop(0, num_peers // group)
        def _(step):
            base = lax.rem(me_row // group + step, num_peers // group) * group
            here = pl.ds(pl.multiple_of(me_slab * total + base * capacity, span), span)
            found = rows_at(first_id_ref[:, here], book_ref[...])
            found = found.astype(jnp.bfloat16).reshape(group, capacity, channels)
            served[pl.ds(base, group)] = found

            @pl.loop(0, group)
            def _(offset):
                peer = base + offset

                @pl.when(peer != me_row)
                def _():
                    target = {"tm": me_slab, "height": peer}
                    push(served.at[peer], answer.at[me_row], 3, target).start()

        own(served, answer, 3, me_row).start()
        load_weight.wait()

        @pl.when(me_row < num_peers - 1)
        def _():
            down().wait_send()
            up().wait_recv()

        @pl.when(me_row > 0)
        def _():
            up().wait_send()
            down().wait_recv()

        last_slab = me_slab + 1 >= slabs
        column = lax.rem(lax.broadcasted_iota(jnp.int32, (pixels, channels), 0), width)

        def forward(image):
            return push(
                hidden.at[image],
                earlier.at[image],
                4,
                {"tm": lax.rem(me_slab + 1, slabs), "height": me_row},
            )

        @pl.loop(0, images)
        def _(image):
            taps = jnp.concatenate([before_ref[image], latent_ref[image], after_ref[image]], axis=0)
            taps = normalize(taps, gain_ref[...])
            windows = [taps[row * width : (row + rows) * width] for row in range(3)]

            def tap(col):
                added = jnp.dot(windows[0], weight_ref[0, col], preferred_element_type=jnp.float32)
                for row in (1, 2):
                    added += jnp.dot(
                        windows[row], weight_ref[row, col], preferred_element_type=jnp.float32
                    )
                return added

            summed = tap(1)
            summed += jnp.where(column == 0, 0.0, pltpu.roll(tap(0), 1, 0))
            summed += jnp.where(column == width - 1, 0.0, pltpu.roll(tap(2), pixels - 1, 0))
            hidden[image] = (summed / (1.0 + jnp.exp(-summed))).astype(jnp.bfloat16)

            @pl.when(jnp.logical_not(last_slab))
            def _():
                forward(image).start()

        load_table.wait()

        @pl.loop(0, members // group)
        def _(step):
            here = pl.ds(pl.multiple_of(step * span, span), span)
            found = rows_at(second_id_ref[:, here], table_ref[...])
            found = found.astype(jnp.bfloat16).reshape(group, capacity, part)
            quants[pl.ds(step * group, group)] = found

        @pl.when(me_slab > 0)
        def _():
            finish(earlier, recv_sems, 4, images)

        @pl.when(me_slab == 0)
        def _():
            earlier[...] = jnp.zeros(earlier.shape, jnp.bfloat16)

        for image in range(images):
            clip, frame = image // frames, image % frames
            mixed = jnp.zeros((pixels, channels), jnp.float32)
            for tap in range(3):
                at = frame - 2 + tap
                frame_ref = hidden if at >= 0 else earlier
                value = frame_ref[clip * frames + at % frames].astype(jnp.float32)
                mixed = mixed + temporal_ref[tap : tap + 1, :] * value
            encoded = latent_ref[image].astype(jnp.float32) + mixed
            flat[image * pixels : (image + 1) * pixels, :] = encoded.astype(jnp.bfloat16)

        def pack(slot_ref, vectors, out):
            @pl.loop(0, num_peers // group)
            def _(step):
                places = step * span + lax.broadcasted_iota(jnp.int32, (span, tokens), 0)
                hot = jnp.where(places == slot_ref[...], 1.0, 0.0).astype(jnp.bfloat16)
                packed = jnp.dot(hot, vectors[...], preferred_element_type=jnp.float32)
                packed = packed.astype(jnp.bfloat16)
                for slab in range(slabs):
                    out[pl.ds(slab * num_peers + step * group, group)] = packed[
                        :, slab * part : (slab + 1) * part
                    ].reshape(group, capacity, part)

        pack(first_slot_ref, flat, first_out)
        send(first_out, first_in, 0)
        own(first_out, first_in, 0, me).start()
        own(served, answer, 3, me_row).wait()
        finish(answer, recv_sems, 3, num_peers - 1)

        @pl.loop(0, tokens // pick_block)
        def _(step):
            here = pl.ds(pl.multiple_of(step * pick_block, pick_block), pick_block)
            quant = rows_at(first_slot_ref[:, here], answer[...].reshape(total, channels))
            residual[here, :] = (flat[here, :].astype(jnp.float32) - quant).astype(jnp.bfloat16)

        pack(second_slot_ref, residual, second_out)
        send(second_out, second_in, 1)
        own(second_out, second_in, 1, me).start()

        def tally(which, id_ref, landing, begin, end):
            ids = id_ref[...]

            @pl.loop(begin, end)
            def _(step):
                start = pl.multiple_of(step * block, block)
                places = start + lax.broadcasted_iota(jnp.int32, (block, amount), 0)
                hot = jnp.where(places == ids, 1.0, 0.0).astype(jnp.bfloat16)
                vectors = landing[...].reshape(amount, part)
                sums_ref[which, pl.ds(start, block), :] = jnp.dot(
                    hot, vectors, preferred_element_type=jnp.float32
                )

        for which, id_ref in ((0, first_id_ref), (1, second_id_ref)):
            ids = id_ref[...]

            @pl.loop(0, blocks)
            def _(step):
                marks = step * block + lax.broadcasted_iota(jnp.int32, (block, amount), 0)
                hot = jnp.where(marks == ids, 1.0, 0.0)
                count_ref[which, step] = jnp.sum(hot, axis=1)[None, :]

        own(first_out, first_in, 0, me).wait()
        finish(first_in, recv_sems, 0, members - 1)
        tally(0, first_id_ref, first_in, 0, blocks)
        own(second_out, second_in, 1, me).wait()
        finish(second_in, recv_sems, 1, members - 1)

        @pl.loop(0, members)
        def _(source):
            leftover = second_in[source].astype(jnp.float32) - quants[source].astype(jnp.float32)
            squares[source] = jnp.sum(leftover * leftover, axis=1)[None, :]

        tally(1, second_id_ref, second_in, 0, 1)
        send(squares, error_ref, 2)
        own(squares, error_ref, 2, me).start()
        tally(1, second_id_ref, second_in, 1, blocks)
        own(squares, error_ref, 2, me).wait()
        finish(error_ref, recv_sems, 2, members - 1)
        finish(first_in, send_sems, 0, members - 1)
        finish(second_in, send_sems, 1, members - 1)
        finish(error_ref, send_sems, 2, members - 1)
        finish(answer, send_sems, 3, num_peers - 1)

        @pl.when(jnp.logical_not(last_slab))
        def _():
            finish(hidden, send_sems, 4, images)

    vmem, anywhere = pl.BlockSpec(memory_space=pltpu.VMEM), pl.BlockSpec(memory_space=pl.ANY)
    bf16 = jnp.bfloat16
    pieces = (members, capacity, part)
    whole_table = part % 128 == 0
    table = codebooks
    if not whole_table:
        start = lax.axis_index("tm") * part
        table = lax.dynamic_slice_in_dim(codebooks[1], start, part, axis=1)
    first_ids, second_ids = got[:, 0].reshape(-1), got[:, 1].reshape(-1)
    return pl.pallas_call(
        kernel,
        out_shape=(
            jax.ShapeDtypeStruct((2, code_rows, part), jnp.float32),
            jax.ShapeDtypeStruct((members, 1, capacity), jnp.float32),
            jax.ShapeDtypeStruct((2, blocks, 1, block), jnp.float32),
        ),
        in_specs=[vmem] * 7 + [anywhere] * 3,
        out_specs=(vmem, vmem, vmem),
        scratch_shapes=[
            pltpu.VMEM(spatial_weight.shape, bf16),
            pltpu.VMEM((code_rows, channels), bf16),
            pltpu.VMEM((code_rows, part), bf16),
            pltpu.VMEM((images, width, channels), bf16),
            pltpu.VMEM((images, width, channels), bf16),
            pltpu.VMEM((num_peers, capacity, channels), bf16),
            pltpu.VMEM((num_peers, capacity, channels), bf16),
            pltpu.VMEM((images, pixels, channels), bf16),
            pltpu.VMEM((images, pixels, channels), bf16),
            pltpu.VMEM((tokens, channels), bf16),
            pltpu.VMEM((tokens, channels), bf16),
            pltpu.VMEM(pieces, bf16),
            pltpu.VMEM(pieces, bf16),
            pltpu.VMEM(pieces, bf16),
            pltpu.VMEM(pieces, bf16),
            pltpu.VMEM(pieces, bf16),
            pltpu.VMEM((members, 1, capacity), jnp.float32),
            pltpu.SemaphoreType.DMA((3,)),
            pltpu.SemaphoreType.DMA((4,)),
            pltpu.SemaphoreType.DMA((7,)),
            pltpu.SemaphoreType.DMA((7,)),
        ],
        compiler_params=pltpu.CompilerParams(
            collective_id=0, has_side_effects=True, vmem_limit_bytes=60 * 2**20
        ),
        name="main",
    )(
        latents.reshape(images, pixels, channels),
        norm_gain[None, :],
        temporal_weight,
        first_ids[None, :],
        second_ids[None, :],
        slots[0][None, :],
        slots[1][None, :],
        spatial_weight,
        codebooks,
        table,
    )


def body(
    latents,
    norm_gain,
    spatial_weight,
    temporal_weight,
    codebooks,
    ema_counts,
    ema_sums,
    decay,
    codes_first,
    codes_second,
):
    channels = latents.shape[-1]
    num_peers = lax.axis_size("height")
    slabs = lax.axis_size("tm")
    part = channels // slabs
    code_rows = codebooks.shape[1]
    amount = codes_first.size
    capacity = 2 * amount // num_peers
    total = num_peers * capacity

    codes = jnp.stack([codes_first.reshape(-1), codes_second.reshape(-1)])
    slots, got = ask(codes, num_peers, slabs, capacity, code_rows)
    sums, squares, counts = main(
        latents,
        norm_gain,
        spatial_weight,
        temporal_weight,
        codebooks,
        got,
        slots,
        slabs,
        num_peers,
        capacity,
    )
    squares = jnp.sum(squares.reshape(slabs, total), axis=0)
    match = slots[1][:, None] == jnp.arange(total, dtype=jnp.int32)[None, :]
    error = jnp.sum(jnp.where(match, squares[None, :], 0.0), axis=1) / channels
    error = error.reshape(codes_first.shape)

    counts = counts.reshape(2, code_rows)
    keep = decay[:, None]
    wide = decay[:, None, None]
    ema_sums_new = wide * ema_sums + (1.0 - wide) * sums
    ema_counts_new = keep * ema_counts + (1.0 - keep) * counts
    return (ema_counts_new, ema_sums_new, error)


def solution(mesh):
    return jax.shard_map(
        body,
        mesh=mesh,
        in_specs=(
            P(None, "tm", "height", None, None),
            P(),
            P(),
            P(),
            P(None, "height", None),
            P(None, "height"),
            P(None, "height", "tm"),
            P(),
            P(None, "tm", "height", None),
            P(None, "tm", "height", None),
        ),
        out_specs=(P(None, "height"), P(None, "height", "tm"), P(None, "tm", "height", None)),
        check_vma=False,
    )
```

```python
import jax
import jax.numpy as jnp
from jax import lax
from jax.experimental import pallas as pl
from jax.experimental.pallas import tpu as pltpu
from jax.sharding import PartitionSpec as P


def normalize(values, norm_gain):
    widened = values.astype(jnp.float32)
    inverse = lax.rsqrt(jnp.mean(widened * widened, axis=-1, keepdims=True) + 1e-06)
    return (widened * inverse * norm_gain).astype(jnp.bfloat16)


def ask(codes, num_peers, slabs, capacity, code_rows):
    amount = codes.shape[1]
    members = slabs * num_peers
    total = num_peers * capacity

    def kernel(code_ref, slot_ref, ids_ref, outgoing, local_sem, send_sem, recv_sem):
        me_row = lax.axis_index("height")
        me = lax.axis_index("tm") * num_peers + me_row

        def peer_of(step):
            peer = lax.rem(me + step, members)
            row = lax.rem(peer, num_peers)
            return row, {"tm": peer // num_peers, "height": row}

        barrier = pltpu.get_barrier_semaphore()

        @pl.loop(1, members)
        def _(step):
            _, target = peer_of(step)
            pl.semaphore_signal(
                barrier, inc=1, device_id=target, device_id_type=pl.DeviceIdType.MESH
            )

        owners = lax.broadcasted_iota(jnp.int32, (num_peers, amount), 0)
        later = lax.broadcasted_iota(jnp.int32, (amount, amount), 1)
        sooner = lax.broadcasted_iota(jnp.int32, (amount, amount), 0)
        order = jnp.where(sooner < later, 1.0, 0.0).astype(jnp.bfloat16)
        for which in range(2):
            code = code_ref[which : which + 1, :]
            local = code - owners * code_rows
            mark = jnp.where((local >= 0) & (local < code_rows), 1.0, 0.0)
            before = jnp.dot(
                mark.astype(jnp.bfloat16), order, preferred_element_type=jnp.float32
            )
            place = mark * (before + (owners * capacity).astype(jnp.float32))
            slot = jnp.sum(place, axis=0, keepdims=True)
            local = jnp.sum(jnp.where(mark > 0.0, local, 0), axis=0, keepdims=True)
            slot_ref[which : which + 1, :] = slot.astype(jnp.int32)
            high = (local // 256).astype(jnp.float32)
            low = (local % 256).astype(jnp.float32)
            kind = lax.broadcasted_iota(jnp.int32, (16, amount), 0)
            digits = jnp.where(kind == 0, high, jnp.where(kind == 1, low, 1.0))
            digits = digits.astype(jnp.bfloat16)
            places = lax.broadcasted_iota(jnp.int32, (total, amount), 0).astype(jnp.float32)
            hot = jnp.where(places == slot, 1.0, 0.0).astype(jnp.bfloat16)
            found = lax.dot_general(
                digits, hot, (((1,), (1,)), ((), ())), preferred_element_type=jnp.float32
            )
            wanted = found[0:1] * 256.0 + found[1:2] + found[2:3] - 1.0
            wanted = wanted.astype(jnp.int32)
            for row in range(num_peers):
                outgoing[row, which : which + 1, :] = wanted[
                    :, row * capacity : (row + 1) * capacity
                ]

        pl.semaphore_wait(barrier, members - 1)

        @pl.loop(1, members)
        def _(step):
            row, target = peer_of(step)
            pltpu.make_async_remote_copy(
                src_ref=outgoing.at[row],
                dst_ref=ids_ref.at[me],
                send_sem=send_sem,
                recv_sem=recv_sem,
                device_id=target,
                device_id_type=pl.DeviceIdType.MESH,
            ).start()

        own = pltpu.make_async_copy(outgoing.at[me_row], ids_ref.at[me], local_sem)
        own.start()
        own.wait()
        most = ids_ref.at[pl.ds(0, members - 1)]
        pltpu.make_async_copy(most, most, recv_sem).wait()
        pltpu.make_async_copy(most, most, send_sem).wait()

    vmem = pl.BlockSpec(memory_space=pltpu.VMEM)
    return pl.pallas_call(
        kernel,
        out_shape=(
            jax.ShapeDtypeStruct(codes.shape, jnp.int32),
            jax.ShapeDtypeStruct((members, 2, capacity), jnp.int32),
        ),
        in_specs=[vmem],
        out_specs=(vmem, vmem),
        scratch_shapes=[
            pltpu.VMEM((num_peers, 2, capacity), jnp.int32),
            pltpu.SemaphoreType.DMA,
            pltpu.SemaphoreType.DMA,
            pltpu.SemaphoreType.DMA,
        ],
        compiler_params=pltpu.CompilerParams(
            collective_id=1, has_side_effects=True, vmem_limit_bytes=60 * 2**20
        ),
        name="ask",
    )(codes)


def block_of(count, limit):
    block = count
    while block > limit and block % 2 == 0:
        block //= 2
    return block


def main(
    latents,
    norm_gain,
    spatial_weight,
    temporal_weight,
    codebooks,
    got,
    slots,
    slabs,
    num_peers,
    capacity,
):
    clips, frames, rows, width, channels = latents.shape
    images, pixels = clips * frames, rows * width
    tokens = images * pixels
    part = channels // slabs
    members, total = slabs * num_peers, num_peers * capacity
    amount = members * capacity
    code_rows = codebooks.shape[1]
    group = block_of(num_peers, 4)
    span = group * capacity
    pick_block = block_of(tokens, 256)
    tally_block = block_of(code_rows, 256)
    block = code_rows
    while block * amount > 2**20 and block % 2 == 0:
        block //= 2
    blocks = code_rows // block

    def kernel(
        latent_ref,
        gain_ref,
        temporal_ref,
        first_id_ref,
        second_id_ref,
        first_slot_ref,
        second_slot_ref,
        weight_hbm,
        book_hbm,
        table_hbm,
        sums_ref,
        error_ref,
        count_ref,
        weight_ref,
        book_ref,
        table_ref,
        before_ref,
        after_ref,
        served,
        answer,
        hidden,
        earlier,
        flat,
        residual,
        first_out,
        second_out,
        first_in,
        second_in,
        quants,
        squares,
        load_sems,
        local_sems,
        send_sems,
        recv_sems,
        turn_sems,
    ):
        me_slab = lax.axis_index("tm")
        me_row = lax.axis_index("height")
        me = me_slab * num_peers + me_row
        load_book = pltpu.make_async_copy(book_hbm.at[0], book_ref, load_sems.at[0])
        load_weight = pltpu.make_async_copy(weight_hbm, weight_ref, load_sems.at[1])
        wanted = table_hbm
        if whole_table:
            lanes = pl.ds(pl.multiple_of(me_slab * part, part), part)
            wanted = table_hbm.at[1, :, lanes]
        load_table = pltpu.make_async_copy(wanted, table_ref, load_sems.at[2])
        load_book.start()
        load_weight.start()
        load_table.start()

        def peer_of(step):
            peer = lax.rem(me + step, members)
            return peer, {"tm": peer // num_peers, "height": lax.rem(peer, num_peers)}

        def push(source, landing, which, target):
            return pltpu.make_async_remote_copy(
                src_ref=source,
                dst_ref=landing,
                send_sem=send_sems.at[which],
                recv_sem=recv_sems.at[which],
                device_id=target,
                device_id_type=pl.DeviceIdType.MESH,
            )

        def send(source, landing, which):
            @pl.loop(1, members)
            def _(step):
                peer, target = peer_of(step)
                push(source.at[peer], landing.at[me], which, target).start()

        def own(source, landing, which, at):
            return pltpu.make_async_copy(source.at[at], landing.at[at], local_sems.at[which])

        def rows_at(ids, table):
            marks = lax.broadcasted_iota(jnp.int32, (table.shape[0], ids.shape[1]), 0)
            hot = jnp.where(marks == ids, 1.0, 0.0).astype(jnp.bfloat16)
            return lax.dot_general(
                hot, table, (((0,), (0,)), ((), ())), preferred_element_type=jnp.float32
            )

        def finish(landing, sems, which, count):
            most = landing.at[pl.ds(0, count)]
            pltpu.make_async_copy(most, most, sems.at[which]).wait()

        barrier = pltpu.get_barrier_semaphore()

        @pl.loop(1, members)
        def _(step):
            _, target = peer_of(step)
            pl.semaphore_signal(
                barrier, inc=1, device_id=target, device_id_type=pl.DeviceIdType.MESH
            )

        @pl.when(me_row == 0)
        def _():
            before_ref[...] = jnp.zeros(before_ref.shape, jnp.bfloat16)

        @pl.when(me_row == num_peers - 1)
        def _():
            after_ref[...] = jnp.zeros(after_ref.shape, jnp.bfloat16)

        pl.semaphore_wait(barrier, members - 1)

        def down():
            target = {"tm": me_slab, "height": lax.rem(me_row + 1, num_peers)}
            return push(latent_ref.at[:, pl.ds(pixels - width, width)], before_ref, 5, target)

        def up():
            target = {"tm": me_slab, "height": lax.rem(me_row + num_peers - 1, num_peers)}
            return push(latent_ref.at[:, pl.ds(0, width)], after_ref, 6, target)

        @pl.when(me_row < num_peers - 1)
        def _():
            down().start()

        @pl.when(me_row > 0)
        def _():
            up().start()

        load_book.wait()

        @pl.loop(0, num_peers // group)
        def _(step):
            base = lax.rem(me_row // group + step, num_peers // group) * group
            here = pl.ds(pl.multiple_of(me_slab * total + base * capacity, span), span)
            found = rows_at(first_id_ref[:, here], book_ref[...])
            found = found.astype(jnp.bfloat16).reshape(group, capacity, channels)
            served[pl.ds(base, group)] = found

            @pl.loop(0, group)
            def _(offset):
                peer = base + offset

                @pl.when(peer != me_row)
                def _():
                    target = {"tm": me_slab, "height": peer}
                    push(served.at[peer], answer.at[me_row], 3, target).start()

        own(served, answer, 3, me_row).start()
        load_weight.wait()

        @pl.when(me_row < num_peers - 1)
        def _():
            down().wait_send()
            up().wait_recv()

        @pl.when(me_row > 0)
        def _():
            up().wait_send()
            down().wait_recv()

        last_slab = me_slab + 1 >= slabs
        column = lax.rem(lax.broadcasted_iota(jnp.int32, (pixels, channels), 0), width)

        def forward(image):
            return push(
                hidden.at[image],
                earlier.at[image],
                4,
                {"tm": lax.rem(me_slab + 1, slabs), "height": me_row},
            )

        @pl.loop(0, images)
        def _(image):
            taps = jnp.concatenate([before_ref[image], latent_ref[image], after_ref[image]], axis=0)
            taps = normalize(taps, gain_ref[...])
            windows = [taps[row * width : (row + rows) * width] for row in range(3)]

            def tap(col):
                added = jnp.dot(windows[0], weight_ref[0, col], preferred_element_type=jnp.float32)
                for row in (1, 2):
                    added += jnp.dot(
                        windows[row], weight_ref[row, col], preferred_element_type=jnp.float32
                    )
                return added

            summed = tap(1)
            summed += jnp.where(column == 0, 0.0, pltpu.roll(tap(0), 1, 0))
            summed += jnp.where(column == width - 1, 0.0, pltpu.roll(tap(2), pixels - 1, 0))
            hidden[image] = (summed / (1.0 + jnp.exp(-summed))).astype(jnp.bfloat16)

            @pl.when(jnp.logical_not(last_slab))
            def _():
                forward(image).start()

        load_table.wait()

        @pl.loop(0, members // group)
        def _(step):
            here = pl.ds(pl.multiple_of(step * span, span), span)
            found = rows_at(second_id_ref[:, here], table_ref[...])
            found = found.astype(jnp.bfloat16).reshape(group, capacity, part)
            quants[pl.ds(step * group, group)] = found

        @pl.when(me_slab > 0)
        def _():
            finish(earlier, recv_sems, 4, images)

        @pl.when(me_slab == 0)
        def _():
            earlier[...] = jnp.zeros(earlier.shape, jnp.bfloat16)

        for image in range(images):
            clip, frame = image // frames, image % frames
            mixed = jnp.zeros((pixels, channels), jnp.float32)
            for tap in range(3):
                at = frame - 2 + tap
                frame_ref = hidden if at >= 0 else earlier
                value = frame_ref[clip * frames + at % frames].astype(jnp.float32)
                mixed = mixed + temporal_ref[tap : tap + 1, :] * value
            encoded = latent_ref[image].astype(jnp.float32) + mixed
            flat[image * pixels : (image + 1) * pixels, :] = encoded.astype(jnp.bfloat16)

        def pack(slot_ref, vectors, out):
            @pl.loop(0, num_peers // group)
            def _(step):
                places = step * span + lax.broadcasted_iota(jnp.int32, (span, tokens), 0)
                hot = jnp.where(places == slot_ref[...], 1.0, 0.0).astype(jnp.bfloat16)
                packed = jnp.dot(hot, vectors[...], preferred_element_type=jnp.float32)
                packed = packed.astype(jnp.bfloat16)
                for slab in range(slabs):
                    out[pl.ds(slab * num_peers + step * group, group)] = packed[
                        :, slab * part : (slab + 1) * part
                    ].reshape(group, capacity, part)

        pack(first_slot_ref, flat, first_out)
        send(first_out, first_in, 0)
        own(first_out, first_in, 0, me).start()
        own(served, answer, 3, me_row).wait()
        finish(answer, recv_sems, 3, num_peers - 1)

        @pl.loop(0, tokens // pick_block)
        def _(step):
            here = pl.ds(pl.multiple_of(step * pick_block, pick_block), pick_block)
            quant = rows_at(first_slot_ref[:, here], answer[...].reshape(total, channels))
            residual[here, :] = (flat[here, :].astype(jnp.float32) - quant).astype(jnp.bfloat16)

        pack(second_slot_ref, residual, second_out)

        for turn in range(slabs):
            slab = lax.rem(me_slab + turn, slabs)

            @pl.loop(1 if turn == 0 else 0, num_peers)
            def _(step):
                row = lax.rem(me_row + step, num_peers)
                pltpu.make_async_remote_copy(
                    src_ref=second_out.at[slab * num_peers + row],
                    dst_ref=second_in.at[me],
                    send_sem=send_sems.at[1],
                    recv_sem=turn_sems.at[turn],
                    device_id={"tm": slab, "height": row},
                    device_id_type=pl.DeviceIdType.MESH,
                ).start()

        own(second_out, second_in, 1, me).start()

        def tally(which, id_ref, landing, turn, begin, end):
            slab = lax.rem(me_slab + slabs - turn, slabs)
            ids = id_ref[:, pl.ds(pl.multiple_of(slab * total, total), total)]

            @pl.loop(begin, end)
            def _(step):
                start = pl.multiple_of(step * tally_block, tally_block)
                places = start + lax.broadcasted_iota(jnp.int32, (tally_block, total), 0)
                hot = jnp.where(places == ids, 1.0, 0.0).astype(jnp.bfloat16)
                vectors = landing[pl.ds(slab * num_peers, num_peers)].reshape(total, part)
                sums = jnp.dot(hot, vectors, preferred_element_type=jnp.float32)
                here = pl.ds(start, tally_block)
                if turn:
                    sums = sums + sums_ref[which, here, :]
                sums_ref[which, here, :] = sums

        for which, id_ref in ((0, first_id_ref), (1, second_id_ref)):
            ids = id_ref[...]

            @pl.loop(0, blocks)
            def _(step):
                marks = step * block + lax.broadcasted_iota(jnp.int32, (block, amount), 0)
                hot = jnp.where(marks == ids, 1.0, 0.0)
                count_ref[which, step] = jnp.sum(hot, axis=1)[None, :]

        own(first_out, first_in, 0, me).wait()
        finish(first_in, recv_sems, 0, members - 1)
        tally_blocks = code_rows // tally_block
        for turn in range(slabs):
            tally(0, first_id_ref, first_in, turn, 0, tally_blocks)
        own(second_out, second_in, 1, me).wait()
        for turn in range(slabs):
            finish(second_in, turn_sems, turn, num_peers - (turn == 0))
            slab = lax.rem(me_slab + slabs - turn, slabs)

            @pl.loop(0, num_peers)
            def _(row):
                source = slab * num_peers + row
                wide = second_in[source].astype(jnp.float32)
                leftover = wide - quants[source].astype(jnp.float32)
                squares[source] = jnp.sum(leftover * leftover, axis=1)[None, :]

            tally(1, second_id_ref, second_in, turn, 0, 1)

            @pl.loop(1 if turn == 0 else 0, num_peers)
            def _(step):
                row = lax.rem(me_row + step, num_peers)
                target = {"tm": slab, "height": row}
                push(squares.at[slab * num_peers + row], error_ref.at[me], 2, target).start()

            if turn == 0:
                own(squares, error_ref, 2, me).start()
            tally(1, second_id_ref, second_in, turn, 1, tally_blocks)

        own(squares, error_ref, 2, me).wait()
        finish(error_ref, recv_sems, 2, members - 1)
        finish(first_in, send_sems, 0, members - 1)
        finish(second_in, send_sems, 1, members - 1)
        finish(error_ref, send_sems, 2, members - 1)
        finish(answer, send_sems, 3, num_peers - 1)

        @pl.when(jnp.logical_not(last_slab))
        def _():
            finish(hidden, send_sems, 4, images)

    vmem, anywhere = pl.BlockSpec(memory_space=pltpu.VMEM), pl.BlockSpec(memory_space=pl.ANY)
    bf16 = jnp.bfloat16
    pieces = (members, capacity, part)
    whole_table = part % 128 == 0
    table = codebooks
    if not whole_table:
        start = lax.axis_index("tm") * part
        table = lax.dynamic_slice_in_dim(codebooks[1], start, part, axis=1)
    first_ids, second_ids = got[:, 0].reshape(-1), got[:, 1].reshape(-1)
    return pl.pallas_call(
        kernel,
        out_shape=(
            jax.ShapeDtypeStruct((2, code_rows, part), jnp.float32),
            jax.ShapeDtypeStruct((members, 1, capacity), jnp.float32),
            jax.ShapeDtypeStruct((2, blocks, 1, block), jnp.float32),
        ),
        in_specs=[vmem] * 7 + [anywhere] * 3,
        out_specs=(vmem, vmem, vmem),
        scratch_shapes=[
            pltpu.VMEM(spatial_weight.shape, bf16),
            pltpu.VMEM((code_rows, channels), bf16),
            pltpu.VMEM((code_rows, part), bf16),
            pltpu.VMEM((images, width, channels), bf16),
            pltpu.VMEM((images, width, channels), bf16),
            pltpu.VMEM((num_peers, capacity, channels), bf16),
            pltpu.VMEM((num_peers, capacity, channels), bf16),
            pltpu.VMEM((images, pixels, channels), bf16),
            pltpu.VMEM((images, pixels, channels), bf16),
            pltpu.VMEM((tokens, channels), bf16),
            pltpu.VMEM((tokens, channels), bf16),
            pltpu.VMEM(pieces, bf16),
            pltpu.VMEM(pieces, bf16),
            pltpu.VMEM(pieces, bf16),
            pltpu.VMEM(pieces, bf16),
            pltpu.VMEM(pieces, bf16),
            pltpu.VMEM((members, 1, capacity), jnp.float32),
            pltpu.SemaphoreType.DMA((3,)),
            pltpu.SemaphoreType.DMA((4,)),
            pltpu.SemaphoreType.DMA((7,)),
            pltpu.SemaphoreType.DMA((7,)),
            pltpu.SemaphoreType.DMA((slabs,)),
        ],
        compiler_params=pltpu.CompilerParams(
            collective_id=0, has_side_effects=True, vmem_limit_bytes=60 * 2**20
        ),
        name="main",
    )(
        latents.reshape(images, pixels, channels),
        norm_gain[None, :],
        temporal_weight,
        first_ids[None, :],
        second_ids[None, :],
        slots[0][None, :],
        slots[1][None, :],
        spatial_weight,
        codebooks,
        table,
    )


def body(
    latents,
    norm_gain,
    spatial_weight,
    temporal_weight,
    codebooks,
    ema_counts,
    ema_sums,
    decay,
    codes_first,
    codes_second,
):
    channels = latents.shape[-1]
    num_peers = lax.axis_size("height")
    slabs = lax.axis_size("tm")
    part = channels // slabs
    code_rows = codebooks.shape[1]
    amount = codes_first.size
    capacity = 2 * amount // num_peers
    total = num_peers * capacity

    codes = jnp.stack([codes_first.reshape(-1), codes_second.reshape(-1)])
    slots, got = ask(codes, num_peers, slabs, capacity, code_rows)
    sums, squares, counts = main(
        latents,
        norm_gain,
        spatial_weight,
        temporal_weight,
        codebooks,
        got,
        slots,
        slabs,
        num_peers,
        capacity,
    )
    squares = jnp.sum(squares.reshape(slabs, total), axis=0)
    match = slots[1][:, None] == jnp.arange(total, dtype=jnp.int32)[None, :]
    error = jnp.sum(jnp.where(match, squares[None, :], 0.0), axis=1) / channels
    error = error.reshape(codes_first.shape)

    counts = counts.reshape(2, code_rows)
    keep = decay[:, None]
    wide = decay[:, None, None]
    ema_sums_new = wide * ema_sums + (1.0 - wide) * sums
    ema_counts_new = keep * ema_counts + (1.0 - keep) * counts
    return (ema_counts_new, ema_sums_new, error)


def solution(mesh):
    return jax.shard_map(
        body,
        mesh=mesh,
        in_specs=(
            P(None, "tm", "height", None, None),
            P(),
            P(),
            P(),
            P(None, "height", None),
            P(None, "height"),
            P(None, "height", "tm"),
            P(),
            P(None, "tm", "height", None),
            P(None, "tm", "height", None),
        ),
        out_specs=(P(None, "height"), P(None, "height", "tm"), P(None, "tm", "height", None)),
        check_vma=False,
    )
```
